32 devices in a mesh: gx: 4 (over z), gy: 2 (over y), gz: 4 (over x, core).
Axes of the slice: x: 2, y: 2, z: 4, core: 2. Of those that a mesh axis runs over, the one named last changes fastest.
Arguments:
- bodies: float32 [1920, 4, 128], P(('gx', 'gy', 'gz'))
- velocity: float32 [1920, 3, 128], P(('gx', 'gy', 'gz')), may hold values from -6 to 6
- select: int32 [32, 5, 16], P(('gx', 'gy', 'gz')), may hold values from 0 to 123, as said below
- pair_target: int32 [32, 1024], P(('gx', 'gy', 'gz')), may hold values from 0 to 59
- pair_source: int32 [32, 1024], P(('gx', 'gy', 'gz')), may hold values from 0 to 139
- counts: int32 [32], P(('gx', 'gy', 'gz')), may hold values from 256 to 1024, as said below
- departures: int32 [32, 12], P(('gx', 'gy', 'gz')), may hold values from 0 to 59, as said below
- owners: int32 [384, 1], P(('gx', 'gy', 'gz')), may hold values from 0 to 3; in each aligned block of 12 rows (0 to 11, 12 to 23, ...) at most 6 rows name the same one
Outputs:
- resident: float32 [1920, 7, 128], P(('gx', 'gy', 'gz'))
- moved_in: float32 [768, 7, 128], P(('gx', 'gy', 'gz'))
The draws below stay inside these ranges and needn't reach their ends.
Inputs may be any that keep to these rules, and one draw needn't show every extreme that they name: `select`: at step k every entry is below 60 + k * 16, and each list names the block 60 + k * 16 - 1. `counts`: some device has 1024 live pairs. `departures`: entries of one device are distinct. `owners`: no owner gets more than 6 blocks from one device, and that many in some devices.
All inputs are finite; a program needn't handle non-finite values.
Results may differ from the reference program's by a relative error of at most 0.0003.
Values sent between devices are 32-bit elements; how exact they have to be, the bound alone decides.
A program may use at most 64 MiB of HBM per device.

```python
import math
import jax
import jax.numpy as jnp
import numpy as np
from jax import lax

BS = 128
OWN = 60
SEND = 16
PMAX = 1024
NBITS = 5
POOL = 140
MOVE = 12
CAP = 6
N_GX = 4
N_GY = 2
N_GZ = 4
DEVICES = 32


def draw_bodies(key, part):
    subkeys = jax.random.split(jax.random.fold_in(key, 101), 2)
    places = jax.random.normal(subkeys[0], (DEVICES * OWN, 3, BS), jnp.float32)
    places = jnp.clip(places, -6.0, 6.0)
    masses = jnp.exp(jax.random.uniform(subkeys[1], (DEVICES * OWN, 1, BS), jnp.float32, jnp.log(0.05), jnp.log(0.5)))
    return jnp.concatenate([places, masses], axis=1).astype(jnp.float32)


def draw_select(key, part):
    subkeys = jax.random.split(jax.random.fold_in(key, 202), 2)
    steps_range = jnp.arange(NBITS, dtype=jnp.int32)
    ceiling = OWN + SEND * steps_range
    raw_draws = jax.random.randint(subkeys[0], (DEVICES, NBITS, SEND), 0, 1 << 30)
    picks = raw_draws % ceiling[None, :, None]
    forced_column = jax.random.randint(subkeys[1], (DEVICES, NBITS, 1), 0, SEND)
    columns = jnp.arange(SEND, dtype=jnp.int32)[None, None, :]
    return jnp.where(columns == forced_column, ceiling[None, :, None] - 1, picks).astype(jnp.int32)


def draw_counts(key, part):
    subkeys = jax.random.split(jax.random.fold_in(key, 303), 2)
    drawn = jax.random.randint(subkeys[0], (DEVICES,), PMAX // 4, PMAX + 1)
    busiest = jax.random.randint(subkeys[1], (), 0, DEVICES)
    return jnp.where(jnp.arange(DEVICES, dtype=jnp.int32) == busiest, PMAX, drawn).astype(jnp.int32)


def draw_departures(key, part):
    subkeys = jax.random.split(jax.random.fold_in(key, 404), DEVICES)
    shuffled = jax.vmap(lambda single: jax.random.permutation(single, OWN))(subkeys)
    return shuffled[:, :MOVE].astype(jnp.int32)


def place_ends(entries, stream_key, low, high):
    place = [jax.random.randint(jax.random.fold_in(stream_key, axis), (), 0, length) for axis, length in enumerate(entries.shape)]
    main_axis = entries.shape.index(max(entries.shape))
    beside = place[:main_axis] + [(place[main_axis] + 1) % entries.shape[main_axis]] + place[main_axis + 1:]
    return entries.at[tuple(place)].set(low).at[tuple(beside)].set(high)


def block_scale(own_key, shape, cuts, smallest, top_value):
    gain = 1.0
    for axis_at, shards_of in cuts:
        steps = jax.random.uniform(jax.random.fold_in(jax.random.fold_in(own_key, 6), axis_at), (shards_of,), jnp.float32, smallest / len(cuts), top_value / len(cuts))
        gain = gain * jnp.repeat(jnp.exp(steps), shape[axis_at] // shards_of).reshape((-1,) + (1,) * (len(shape) - 1 - axis_at))
    return gain


def deal_out(own_key, own, number, rows, amount, top, reach, lean):
    ranking = jax.random.permutation(own_key, amount)
    crowded, common = portions_of(amount, rows * top, reach, lean, True), portions_of(amount, rows * top, reach, lean, False)
    places = jnp.arange(amount)

    def named(lengths, rotation):
        used = int((lengths > 0).sum())
        fixed = max(1, used // 4)
        passed = fixed + (places - fixed + rotation * (used - fixed)) % max(1, amount - fixed)
        return jnp.zeros((amount,), jnp.int32).at[ranking[jnp.where(places < fixed, places, passed)]].set(jnp.asarray(lengths, jnp.int32))

    lengths = jnp.where(number % 4 == 0, named(crowded, number // 4), named(common, number - number // 4 - 1))
    mixed = jax.random.permutation(jax.random.fold_in(own, 3), amount)
    giver, taker = mixed[0:amount // 2 * 2:2], mixed[1:amount // 2 * 2:2]
    margin = jnp.minimum(lengths[giver] - 1, reach - lengths[taker]) // 2
    margin = jnp.where((giver == ranking[0]) | (taker == ranking[0]) | (lengths[taker] == 0), 0, jnp.maximum(margin, 0))
    passed = jax.random.randint(jax.random.fold_in(own, 4), (amount // 2,), 0, 1 << 20) % (margin + 1)
    lengths = lengths.at[giver].add(-passed).at[taker].add(passed)
    items = jnp.searchsorted(jnp.cumsum(lengths), jnp.arange(rows * top), side="right").astype(jnp.int32)
    table = items.reshape(top, rows).T
    table = table[jax.random.permutation(jax.random.fold_in(own, 1), rows)]
    rotation = jax.random.randint(jax.random.fold_in(own, 2), (rows, 1), 0, top)
    return jnp.take_along_axis(table, (jnp.arange(top)[None, :] + rotation) % top, axis=1)


def portions_of(number_of, total, limit, skew, full):
    loads = [(1 << 20) // math.isqrt(standing ** skew) + 1 for standing in range(1, number_of + 1)]
    largest = limit if full else min(limit, max(-(-total // number_of), total * loads[0] // sum(loads)))
    least = 1 if total - largest >= number_of - 1 else 0
    given, surplus = [largest] + [least] * (number_of - 1), total - largest - least * (number_of - 1)
    while surplus > 0:
        candidates = [i for i in range(1, number_of) if given[i] < largest] or [i for i in range(1, number_of) if given[i] < limit]
        whole, remaining = sum([loads[i] for i in candidates]), surplus
        for i in candidates:
            addition = min(limit - given[i], max(1, remaining * loads[i] // whole), surplus)
            given[i] = given[i] + addition
            surplus = surplus - addition
    return np.array(given)


def noise(key, shape, width, bound, cuts=(), held_as=jnp.bfloat16):
    factor_of = block_scale(key, shape, cuts, -0.22, 0.18) if cuts else 1.0
    result = jax.random.normal(key, shape, jnp.float32) * width * factor_of
    return jnp.minimum(jnp.maximum(result, -bound), bound).astype(held_as)


def setup_inputs(seed: int = 0) -> dict:
    streams_of = jax.random.split(jax.random.key(seed), 9)
    bodies = draw_bodies(jax.random.fold_in(streams_of[8], 71), 0)
    velocity = noise(streams_of[1], (DEVICES * OWN, 3, BS), 1.0, 6.0, ((0, 32),), jnp.float32)
    select = draw_select(jax.random.fold_in(streams_of[8], 71), 0)
    pair_target = place_ends(jax.random.randint(streams_of[3], (DEVICES, PMAX), 0, OWN), jax.random.fold_in(streams_of[3], 1), 0, OWN - 1).astype(jnp.int32)
    pair_source = place_ends(jax.random.randint(streams_of[4], (DEVICES, PMAX), 0, POOL), jax.random.fold_in(streams_of[4], 1), 0, POOL - 1).astype(jnp.int32)
    counts = draw_counts(jax.random.fold_in(streams_of[8], 71), 0)
    departures = draw_departures(jax.random.fold_in(streams_of[8], 71), 0)
    owners_keys = jax.random.split(jax.random.fold_in(streams_of[7], 1), (DEVICES * MOVE) // MOVE)
    owners_turns = jax.random.permutation(jax.random.fold_in(streams_of[7], 3), (DEVICES * MOVE) // MOVE)
    owners = jax.vmap(lambda own, number: deal_out(jax.random.fold_in(streams_of[7], 2), own, number, MOVE, N_GZ, 1, CAP, 1))(owners_keys, owners_turns).reshape((DEVICES * MOVE, 1))
    return dict(bodies=bodies, velocity=velocity, select=select, pair_target=pair_target, pair_source=pair_source, counts=counts, departures=departures, owners=owners)


soften = 0.01
timestep = 0.25
group_rows = 64

def block_forces(targets, sources, validity):
    delta_x = sources[:, 0, None, :] - targets[:, 0, :, None]
    offset_vertical = sources[:, 1, None, :] - targets[:, 1, :, None]
    delta_z = sources[:, 2, None, :] - targets[:, 2, :, None]
    radius_sq = delta_x * delta_x + offset_vertical * offset_vertical + delta_z * delta_z + soften
    weight = sources[:, 3, None, :] * lax.rsqrt(radius_sq) / radius_sq
    pull_sums = jnp.stack([lax.optimization_barrier(jnp.sum(delta_x * weight, axis=2)), lax.optimization_barrier(jnp.sum(offset_vertical * weight, axis=2)), lax.optimization_barrier(jnp.sum(delta_z * weight, axis=2))], axis=1)
    return pull_sums * validity[:, None, None]

def axis_bits(extent):
    return extent.bit_length() - 1

def reference(bodies, velocity, select, pair_target, pair_source, counts, departures, owners):
    bits_gx = axis_bits(N_GX)
    bits_gy = axis_bits(N_GY)
    bits_gz = axis_bits(N_GZ)
    every_device_list = jnp.arange(DEVICES, dtype=jnp.int32)
    anchor = every_device_list[:, None] * OWN + jnp.arange(OWN, dtype=jnp.int32)[None, :]
    flip_masks = [1 << bits_gz + bits_gy + bit_index for bit_index in range(bits_gx)]
    flip_masks = flip_masks + [1 << bits_gz + bit_index for bit_index in range(bits_gy)]
    flip_masks = flip_masks + [1 << bit_index for bit_index in range(bits_gz)]
    for step_index, flip_mask in enumerate(flip_masks):
        partner = jnp.bitwise_xor(every_device_list, flip_mask)
        picked = jnp.take_along_axis(anchor, select[:, step_index, :], axis=1)
        anchor = jnp.concatenate([anchor, picked[partner]], axis=1)
    source_ids = jnp.take_along_axis(anchor, pair_source, axis=1).astype(jnp.int32)
    target_ids = (every_device_list[:, None] * OWN + pair_target).astype(jnp.int32)
    in_range = (jnp.arange(PMAX, dtype=jnp.int32)[None, :] < counts[:, None]).astype(jnp.float32)
    members = jnp.arange(OWN, dtype=jnp.int32)
    groups = PMAX // group_rows

    def device_accel(pieces):
        target_rows, source_rows, validity, local_rows = pieces

        def add_group(running, group):
            target_group, source_group, valid_group, local_group = group
            pull_sums = block_forces(bodies[target_group], bodies[source_group], valid_group)
            onehot = (local_group[:, None] == members[None, :]).astype(jnp.float32)
            return (running + jnp.einsum('gk,gcb->kcb', onehot, pull_sums, precision=lax.Precision.HIGHEST), None)
        grouped = (target_rows.reshape(groups, group_rows), source_rows.reshape(groups, group_rows), validity.reshape(groups, group_rows), local_rows.reshape(groups, group_rows))
        total, _ = lax.scan(add_group, jnp.zeros((OWN, 3, BS), jnp.float32), grouped)
        return total
    accelerations = lax.map(device_accel, (target_ids, source_ids, in_range, pair_target))
    accelerations = accelerations.reshape(DEVICES * OWN, 3, BS)
    velocity_new = velocity + timestep * accelerations
    position = bodies[:, :3, :] + timestep * velocity_new
    refreshed_state = jnp.concatenate([position, bodies[:, 3:4, :], velocity_new], axis=1)
    updated_dev = refreshed_state.reshape(DEVICES, OWN, 7, BS)
    departed = jnp.any(members[None, :, None] == departures[:, None, :], axis=2)
    resident = jnp.where(departed[:, :, None, None], jnp.zeros_like(updated_dev), updated_dev).reshape(DEVICES * OWN, 7, BS)
    owner_rows = owners.reshape(DEVICES, MOVE)
    same_owner = owner_rows[:, :, None] == owner_rows[:, None, :]
    moves = jnp.arange(MOVE, dtype=jnp.int32)
    prior_positions = moves[None, :] < moves[:, None]
    place_slot_index = lax.optimization_barrier(jnp.sum((same_owner & prior_positions[None, :, :]).astype(jnp.int32), axis=2))
    body_routes_table = ((owner_rows[:, :, None, None] == jnp.arange(N_GZ, dtype=jnp.int32)[None, None, :, None]) & (place_slot_index[:, :, None, None] == jnp.arange(CAP, dtype=jnp.int32)[None, None, None, :])).astype(jnp.float32)
    leaving = updated_dev[every_device_list[:, None], departures]
    outbox = jnp.einsum('dmgc,dmrb->dgcrb', body_routes_table, leaving, precision=lax.Precision.HIGHEST)
    outbox = outbox.reshape(DEVICES // N_GZ, N_GZ, N_GZ, CAP, 7, BS)
    moved_in = jnp.swapaxes(outbox, 1, 2).reshape(DEVICES * N_GZ * CAP, 7, BS)
    return (resident, moved_in)
```

```python
import functools
import math

import jax
import jax.numpy as jnp
from jax import lax
from jax.experimental import pallas as pl
from jax.experimental.pallas import tpu as pltpu
from jax.sharding import PartitionSpec as P

soften = 0.01
timestep = 0.25
deepest_unroll = 64
coarse = 2.0**14.5


def exchange_kernel(steps, select_ref, bodies_ref, pool_ref, outgoing, arriving, send_sem, recv_sem):
    own_blocks = bodies_ref.shape[0]
    send_count = outgoing.shape[1]
    partners = []
    for axis, stride in steps:
        me = lax.axis_index(axis)
        side = lax.rem(me // stride, 2)
        partners.append({axis: me + (1 - 2 * side) * stride})
    barrier = pltpu.get_barrier_semaphore()
    for partner in partners:
        pl.semaphore_signal(
            barrier, inc=1, device_id=partner, device_id_type=pl.DeviceIdType.MESH
        )
    pool_ref[0:own_blocks] = bodies_ref[...]
    pl.semaphore_wait(barrier, len(partners))
    copies = []
    for k, partner in enumerate(partners):
        for j in range(send_count):
            outgoing[k, j] = pool_ref[select_ref[k, 0, j]]
        copy = pltpu.make_async_remote_copy(
            src_ref=outgoing.at[k],
            dst_ref=arriving.at[k],
            send_sem=send_sem.at[k],
            recv_sem=recv_sem.at[k],
            device_id=partner,
            device_id_type=pl.DeviceIdType.MESH,
        )
        copy.start()
        copies.append(copy)
        copy.wait_recv()
        base = own_blocks + k * send_count
        pool_ref[base : base + send_count] = arriving[k]
    for copy in copies:
        copy.wait_send()


def split(values):
    high = values.astype(jnp.bfloat16).astype(jnp.float32)
    rest = values - high
    middle = rest.astype(jnp.bfloat16).astype(jnp.float32)
    return high, middle, rest - middle


def frame_of(own_ref):
    lowest = jnp.min(own_ref[...], axis=0)
    highest = jnp.max(own_ref[...], axis=0)
    lowest = jnp.min(lowest, axis=1, keepdims=True)
    highest = jnp.max(highest, axis=1, keepdims=True)
    place = lax.broadcasted_iota(jnp.int32, lowest.shape, 0) < 3
    centre = jnp.where(place, 0.5 * lowest + 0.5 * highest, 0.0)
    reach = jnp.where(place, 0.5 * highest - 0.5 * lowest, 0.0)
    reach = jnp.max(reach, axis=0, keepdims=True)
    return centre, reach * coarse


def coordinates(block, centre):
    place = lax.broadcasted_iota(jnp.int32, block.shape, 0) < 3
    return jnp.where(place, block - centre, 0.0)


def pieces_of(x, grid, extra):
    coarse_x = (x + grid) - grid
    fine_x = x - coarse_x
    g1 = coarse_x.astype(jnp.bfloat16).astype(jnp.float32)
    g2 = coarse_x - g1
    f1 = fine_x.astype(jnp.bfloat16).astype(jnp.float32)
    f2 = fine_x - f1
    norm = jnp.sum(coarse_x * coarse_x, axis=0, keepdims=True)
    rest = jnp.sum(fine_x * (2.0 * coarse_x + fine_x), axis=0, keepdims=True) + extra
    return (g1, g2, f1, f2), (*split(norm), *split(rest))


meetings = ((0, 0), (0, 1), (1, 0), (1, 1), (0, 2), (2, 0), (1, 2), (2, 1), (0, 3), (3, 0), (1, 3), (3, 1), (2, 2), (2, 3), (3, 2))


def rows_of(pieces, norms, source):
    place = lax.broadcasted_iota(jnp.int32, pieces[0].shape, 0) < 3
    one = jnp.ones_like(norms[0])
    rows = []
    for n, (from_source, from_target) in enumerate(meetings):
        if n >= 2 * len(norms):
            fill = jnp.zeros_like(one)
        elif (n % 2 == 0) == source:
            fill = norms[n // 2]
        else:
            fill = one
        mine = pieces[from_source] if source else -2.0 * pieces[from_target]
        rows.append(jnp.where(place, mine, fill))
    rows.append(jnp.zeros_like(rows[0]))
    return jnp.concatenate(rows, axis=0)


def source_features(block, centre, grid):
    x = coordinates(block, centre)
    features = rows_of(*pieces_of(x, grid, 0.0), True).T.astype(jnp.bfloat16)
    mass = block[3:4]
    place = lax.broadcasted_iota(jnp.int32, block.shape, 0) < 3
    pulls = split(jnp.where(place, x * mass, mass))
    pulls = jnp.concatenate([*pulls, jnp.zeros_like(x)], axis=0).astype(jnp.bfloat16)
    return features, pulls


def target_features(block, centre, grid):
    x = coordinates(block, centre)
    return rows_of(*pieces_of(x, grid, soften), False).astype(jnp.bfloat16)


def pair_pull(source, target, pulls):
    distance = jnp.dot(source, target, preferred_element_type=jnp.float32)
    inverse = lax.rsqrt(jnp.maximum(distance, soften))
    w = inverse * inverse * inverse
    high = w.astype(jnp.bfloat16)
    low = (w - high.astype(jnp.float32)).astype(jnp.bfloat16)
    return jnp.dot(
        jnp.concatenate([pulls, pulls], axis=1),
        jnp.concatenate([high, low], axis=0),
        preferred_element_type=jnp.float32,
    )


def step_kernel(
    slot_total,
    target_ref,
    source_ref,
    count_ref,
    departures_ref,
    owners_ref,
    pool_ref,
    velocity_ref,
    resident_ref,
    outbox_ref,
    sources,
    pulls,
    targets,
    sums,
    used,
):
    pool_size = pool_ref.shape[0]
    own_blocks = velocity_ref.shape[1]
    span = pool_ref.shape[2]
    unroll = math.gcd(target_ref.shape[0], deepest_unroll)

    centre, grid = frame_of(pool_ref.at[0:own_blocks])
    batch = math.gcd(pool_size, 10)

    @pl.loop(0, pool_size // batch)
    def _(group):
        for b in [group * batch + u for u in range(batch)]:
            sources[b], pulls[b] = source_features(pool_ref[b], centre, grid)

    own_batch = math.gcd(own_blocks, 12)

    @pl.loop(0, own_blocks // own_batch)
    def _(group):
        for b in [group * own_batch + u for u in range(own_batch)]:
            targets[b] = target_features(pool_ref[b], centre, grid)

    sums[...] = jnp.zeros_like(sums)

    @pl.loop(0, (count_ref[0] + unroll - 1) // unroll)
    def _(group):
        for u in range(unroll):
            p = group * unroll + u
            t = target_ref[p]
            s = source_ref[p]
            where = jnp.where(p < count_ref[0], t, own_blocks)
            sums[where] += pair_pull(sources[s], targets[t], pulls[s])

    @pl.loop(0, own_blocks // own_batch)
    def _(group):
        for b in [group * own_batch + u for u in range(own_batch)]:
            row = pl.ds(b, 1)
            total = sums[b, 0:4] + sums[b, 4:8] + sums[b, 8:12]
            block = pool_ref[b]
            pull = total - coordinates(block, centre) * total[3:4]
            for c in range(3):
                velocity_new = velocity_ref[c, row, :] + timestep * pull[c : c + 1]
                resident_ref[c, row, :] = block[c : c + 1, :] + timestep * velocity_new
                resident_ref[4 + c, row, :] = velocity_new
            resident_ref[3, row, :] = block[3:4, :]

    outbox_ref[...] = jnp.zeros_like(outbox_ref)
    for g in range(used.shape[0]):
        used[g] = 0
    for m in range(departures_ref.shape[0]):
        d = departures_ref[m]
        owner = owners_ref[m]
        slot = used[owner]
        used[owner] = slot + 1
        for c in range(resident_ref.shape[0]):
            outbox_ref[owner * slot_total + slot, c : c + 1, :] = resident_ref[c, pl.ds(d, 1), :]
            resident_ref[c, pl.ds(d, 1), :] = jnp.zeros((1, span), jnp.float32)


def on_device(bodies, velocity, select, pair_target, pair_source, counts, departures, owners):
    own_blocks = bodies.shape[0]
    span = bodies.shape[2]
    smem = pl.BlockSpec(memory_space=pltpu.SMEM)
    vmem = pl.BlockSpec(memory_space=pltpu.VMEM)
    steps = [
        (axis, 2**bit)
        for axis in ("gx", "gy", "gz")
        for bit in range(lax.axis_size(axis).bit_length() - 1)
    ]
    send_count = select.shape[2]
    slab = pltpu.VMEM((len(steps), send_count, 4, span), jnp.float32)
    pool = pl.pallas_call(
        functools.partial(exchange_kernel, steps),
        out_shape=jax.ShapeDtypeStruct((own_blocks + len(steps) * send_count, 4, span), jnp.float32),
        in_specs=[smem, vmem],
        out_specs=vmem,
        scratch_shapes=[
            slab,
            slab,
            pltpu.SemaphoreType.DMA((len(steps),)),
            pltpu.SemaphoreType.DMA((len(steps),)),
        ],
        compiler_params=pltpu.CompilerParams(collective_id=0, has_side_effects=True),
        name="exchange",
    )(jnp.transpose(select, (1, 0, 2)), bodies)
    group_size = lax.axis_size("gz")
    move_count = departures.shape[1]
    slot_total = max(2, 2 * move_count // group_size)
    resident, outbox = pl.pallas_call(
        functools.partial(step_kernel, slot_total),
        out_shape=(
            jax.ShapeDtypeStruct((7, own_blocks, span), jnp.float32),
            jax.ShapeDtypeStruct((group_size * slot_total, 7, span), jnp.float32),
        ),
        in_specs=[smem] * 5 + [vmem] * 2,
        out_specs=(vmem, vmem),
        scratch_shapes=[
            pltpu.VMEM((pool.shape[0], span, 64), jnp.bfloat16),
            pltpu.VMEM((pool.shape[0], 16, span), jnp.bfloat16),
            pltpu.VMEM((own_blocks, 64, span), jnp.bfloat16),
            pltpu.VMEM((own_blocks + 1, 16, span), jnp.float32),
            pltpu.SMEM((group_size,), jnp.int32),
        ],
        compiler_params=pltpu.CompilerParams(vmem_limit_bytes=48 << 20),
        name="gravity",
    )(
        pair_target[0],
        pair_source[0],
        counts,
        departures[0],
        owners[:, 0],
        pool,
        jnp.transpose(velocity, (1, 0, 2)),
    )
    arrived = lax.all_to_all(
        outbox.reshape(group_size, slot_total, 7, span), "gz", split_axis=0, concat_axis=0, tiled=True
    )
    return jnp.transpose(resident, (1, 0, 2)), arrived.reshape(group_size * slot_total, 7, span)


def solution(mesh):
    everywhere = ("gx", "gy", "gz")
    cube = P(everywhere, None, None)
    flat = P(everywhere, None)
    return jax.shard_map(
        on_device,
        mesh=mesh,
        in_specs=(cube, cube, cube, flat, flat, P(everywhere), flat, flat),
        out_specs=(cube, cube),
        check_vma=False,
    )
```

```python
import functools
import math

import jax
import jax.numpy as jnp
from jax import lax
from jax.experimental import pallas as pl
from jax.experimental.pallas import tpu as pltpu
from jax.sharding import PartitionSpec as P

soften = 0.01
timestep = 0.25
deepest_unroll = 64
early_unroll = 32
coarse = 2.0**14.5


def split(values):
    high = values.astype(jnp.bfloat16).astype(jnp.float32)
    rest = values - high
    middle = rest.astype(jnp.bfloat16).astype(jnp.float32)
    return high, middle, rest - middle


def frame_of(own_ref):
    lowest = jnp.min(own_ref[...], axis=0)
    highest = jnp.max(own_ref[...], axis=0)
    lowest = jnp.min(lowest, axis=1, keepdims=True)
    highest = jnp.max(highest, axis=1, keepdims=True)
    place = lax.broadcasted_iota(jnp.int32, lowest.shape, 0) < 3
    centre = jnp.where(place, 0.5 * lowest + 0.5 * highest, 0.0)
    reach = jnp.where(place, 0.5 * highest - 0.5 * lowest, 0.0)
    reach = jnp.max(reach, axis=0, keepdims=True)
    return centre, reach * coarse


def coordinates(block, centre):
    place = lax.broadcasted_iota(jnp.int32, block.shape, 0) < 3
    return jnp.where(place, block - centre, 0.0)


def pieces_of(x, grid, extra):
    coarse_x = (x + grid) - grid
    fine_x = x - coarse_x
    g1 = coarse_x.astype(jnp.bfloat16).astype(jnp.float32)
    g2 = coarse_x - g1
    f1 = fine_x.astype(jnp.bfloat16).astype(jnp.float32)
    f2 = fine_x - f1
    norm = jnp.sum(coarse_x * coarse_x, axis=0, keepdims=True)
    rest = jnp.sum(fine_x * (2.0 * coarse_x + fine_x), axis=0, keepdims=True) + extra
    return (g1, g2, f1, f2), (*split(norm), *split(rest))


meetings = ((0, 0), (0, 1), (1, 0), (1, 1), (0, 2), (2, 0), (1, 2), (2, 1), (0, 3), (3, 0), (1, 3), (3, 1), (2, 2), (2, 3), (3, 2))


def rows_of(pieces, norms, source):
    place = lax.broadcasted_iota(jnp.int32, pieces[0].shape, 0) < 3
    one = jnp.ones_like(norms[0])
    rows = []
    for n, (from_source, from_target) in enumerate(meetings):
        if n >= 2 * len(norms):
            fill = jnp.zeros_like(one)
        elif (n % 2 == 0) == source:
            fill = norms[n // 2]
        else:
            fill = one
        mine = pieces[from_source] if source else -2.0 * pieces[from_target]
        rows.append(jnp.where(place, mine, fill))
    rows.append(jnp.zeros_like(rows[0]))
    return jnp.concatenate(rows, axis=0)


def source_features(block, centre, grid):
    x = coordinates(block, centre)
    features = rows_of(*pieces_of(x, grid, 0.0), True).T.astype(jnp.bfloat16)
    mass = block[3:4]
    place = lax.broadcasted_iota(jnp.int32, block.shape, 0) < 3
    pulls = split(jnp.where(place, x * mass, mass))
    pulls = jnp.concatenate([*pulls, jnp.zeros_like(x)], axis=0).astype(jnp.bfloat16)
    return features, pulls


def target_features(block, centre, grid):
    x = coordinates(block, centre)
    return rows_of(*pieces_of(x, grid, soften), False).astype(jnp.bfloat16)


def pair_pull(source, target, pulls):
    distance = jnp.dot(source, target, preferred_element_type=jnp.float32)
    inverse = lax.rsqrt(jnp.maximum(distance, soften))
    w = inverse * inverse * inverse
    high = w.astype(jnp.bfloat16)
    low = (w - high.astype(jnp.float32)).astype(jnp.bfloat16)
    return jnp.dot(
        jnp.concatenate([pulls, pulls], axis=1),
        jnp.concatenate([high, low], axis=0),
        preferred_element_type=jnp.float32,
    )


def own_first(target_ref, source_ref, count, own_blocks):
    rows, lanes = target_ref.shape
    total = rows * lanes
    place = lanes * lax.broadcasted_iota(jnp.int32, (rows, lanes), 0) + lax.broadcasted_iota(jnp.int32, (rows, lanes), 1)
    own = (source_ref[...] < own_blocks) & (place < count)
    before = lax.broadcasted_iota(jnp.int32, (lanes, lanes), 0) <= lax.broadcasted_iota(jnp.int32, (lanes, lanes), 1)
    running = jnp.dot(
        jnp.where(own, 1.0, 0.0).astype(jnp.bfloat16),
        jnp.where(before, 1.0, 0.0).astype(jnp.bfloat16),
        preferred_element_type=jnp.float32,
    )
    ends = running[:, lanes - 1 : lanes]
    own_total = jnp.sum(ends, axis=0, keepdims=True)
    earlier = lax.broadcasted_iota(jnp.int32, (rows, rows), 1) < lax.broadcasted_iota(jnp.int32, (rows, rows), 0)
    offsets = jnp.dot(
        jnp.where(earlier, 1.0, 0.0).astype(jnp.bfloat16),
        jnp.broadcast_to(ends, (rows, lanes)).astype(jnp.bfloat16),
        preferred_element_type=jnp.float32,
    )
    running = running + offsets
    slot = jnp.where(own, running - 1.0, own_total + place.astype(jnp.float32) - running).T
    digits = []
    for values in (target_ref[...], source_ref[...]):
        digits += [(values // 128).astype(jnp.float32), (values % 128).astype(jnp.float32)]
    moved = jnp.zeros((8, total), jnp.float32)
    lane = lax.broadcasted_iota(jnp.int32, (lanes, total), 1).astype(jnp.float32)
    for r in range(rows):
        values = jnp.concatenate([d[r : r + 1] for d in digits] + [jnp.zeros((4, lanes), jnp.float32)], axis=0)
        here = jnp.where(slot[:, r : r + 1] == lane, 1.0, 0.0).astype(jnp.bfloat16)
        moved = moved + jnp.dot(values.astype(jnp.bfloat16), here, preferred_element_type=jnp.float32)
    targets = 128.0 * moved[0:1] + moved[1:2]
    sources = 128.0 * moved[2:3] + moved[3:4]
    return targets, sources, own_total


def early_groups(steps, limit):
    plan = []
    for k, (axis, stride) in enumerate(steps):
        groups = 0 if (axis, stride) == ("gz", 1) else 2 if k == 0 else 4
        plan.append(min(groups, limit - sum(plan)))
    return plan


def exchange_kernel(
    steps,
    plan,
    select_ref,
    count_ref,
    target_ref,
    source_ref,
    bodies_ref,
    pool_ref,
    sums_ref,
    order_ref,
    outgoing,
    arriving,
    sources,
    pulls,
    targets,
    parts,
    order,
    send_sem,
    recv_sem,
    order_sem,
):
    own_blocks = bodies_ref.shape[0]
    send_count = outgoing.shape[1]
    partners = []
    for axis, stride in steps:
        me = lax.axis_index(axis)
        side = lax.rem(me // stride, 2)
        partners.append({axis: me + (1 - 2 * side) * stride})
    barrier = pltpu.get_barrier_semaphore()
    for partner in partners:
        pl.semaphore_signal(
            barrier, inc=1, device_id=partner, device_id_type=pl.DeviceIdType.MESH
        )
    pool_ref[0:own_blocks] = bodies_ref[...]
    centre, grid = frame_of(bodies_ref)
    batch = math.gcd(own_blocks, 12)

    @pl.loop(0, own_blocks // batch)
    def _(group):
        for b in [group * batch + u for u in range(batch)]:
            sources[b], pulls[b] = source_features(bodies_ref[b], centre, grid)
            targets[b] = target_features(bodies_ref[b], centre, grid)

    def work(first, groups):
        @pl.loop(first, first + groups)
        def _(group):
            for u in range(early_unroll):
                p = group * early_unroll + u
                t = jnp.clip(order[0, p], 0, own_blocks - 1)
                s = jnp.clip(order[1, p], 0, own_blocks - 1)
                pull = pair_pull(sources[s], targets[t], pulls[s])
                parts[p] = pull[0:8] + pull[8:16]

    pl.semaphore_wait(barrier, len(partners))
    copies = []
    done = 0
    for k, partner in enumerate(partners):
        for j in range(send_count):
            outgoing[k, j] = pool_ref[select_ref[k, 0, j]]
        copy = pltpu.make_async_remote_copy(
            src_ref=outgoing.at[k],
            dst_ref=arriving.at[k],
            send_sem=send_sem.at[k],
            recv_sem=recv_sem.at[k],
            device_id=partner,
            device_id_type=pl.DeviceIdType.MESH,
        )
        copy.start()
        copies.append(copy)
        if k == 0:
            row_t, row_s, own_total = own_first(target_ref, source_ref, count_ref[0], own_blocks)
            table = jnp.concatenate(
                [row_t, row_s, jnp.broadcast_to(own_total, row_t.shape), jnp.zeros((5, row_t.shape[1]), jnp.float32)], axis=0
            )
            order_ref[...] = table.astype(jnp.int32)
            into_order = pltpu.make_async_copy(order_ref, order, order_sem)
            into_order.start()
            into_order.wait()
        if plan[k] > 0:
            work(done, plan[k])
            done += plan[k]
        if k == len(partners) - 1:
            early = parts.shape[0]
            members = lax.broadcasted_iota(jnp.int32, (-(-own_blocks // 16) * 16, early), 0)
            spot = lax.broadcasted_iota(jnp.int32, members.shape, 1).astype(jnp.float32)
            chosen = (members == order_ref[0:1, 0:early]) & (spot < own_total)
            chosen = jnp.where(chosen, 1.0, 0.0).astype(jnp.bfloat16)
            for c in range(4):
                total = jnp.zeros((members.shape[0], parts.shape[2]), jnp.float32)
                for piece in split(parts[:, c, :] + parts[:, c + 4, :]):
                    total = total + jnp.dot(chosen, piece.astype(jnp.bfloat16), preferred_element_type=jnp.float32)
                sums_ref[:, c, :] = total[0:own_blocks]
        copy.wait_recv()
        base = own_blocks + k * send_count
        pool_ref[base : base + send_count] = arriving[k]
    for copy in copies:
        copy.wait_send()


def step_kernel(
    slot_total,
    early,
    order_ref,
    count_ref,
    departures_ref,
    owners_ref,
    pool_ref,
    early_sums_ref,
    velocity_ref,
    resident_ref,
    outbox_ref,
    sources,
    pulls,
    targets,
    sums,
    used,
):
    pool_size = pool_ref.shape[0]
    own_blocks = velocity_ref.shape[1]
    span = pool_ref.shape[2]
    slots = order_ref.shape[1]
    unroll = math.gcd(slots, deepest_unroll)
    own_total = order_ref[2, 0]
    first = jnp.minimum(own_total, early)

    centre, grid = frame_of(pool_ref.at[0:own_blocks])

    def prepare(start, stop):
        batch = math.gcd(stop - start, 10)

        @pl.loop(0, (stop - start) // batch)
        def _(group):
            for b in [start + group * batch + u for u in range(batch)]:
                sources[b], pulls[b] = source_features(pool_ref[b], centre, grid)

    prepare(own_blocks, pool_size)

    @pl.when(own_total > early)
    def _():
        prepare(0, own_blocks)

    own_batch = math.gcd(own_blocks, 12)

    @pl.loop(0, own_blocks // own_batch)
    def _(group):
        for b in [group * own_batch + u for u in range(own_batch)]:
            targets[b] = target_features(pool_ref[b], centre, grid)

    sums[0:own_blocks, 0:4] = early_sums_ref[...]
    sums[0:own_blocks, 4:16] = jnp.zeros((own_blocks, 12, span), jnp.float32)
    sums[own_blocks] = jnp.zeros(sums.shape[1:], jnp.float32)

    @pl.loop(0, (count_ref[0] - first + unroll - 1) // unroll)
    def _(group):
        for u in range(unroll):
            p = first + group * unroll + u
            live = p < count_ref[0]
            p = jnp.minimum(p, slots - 1)
            t = order_ref[0, p]
            s = order_ref[1, p]
            where = jnp.where(live, t, own_blocks)
            sums[where] += pair_pull(sources[s], targets[t], pulls[s])

    @pl.loop(0, own_blocks // own_batch)
    def _(group):
        for b in [group * own_batch + u for u in range(own_batch)]:
            row = pl.ds(b, 1)
            total = sums[b, 0:4] + sums[b, 4:8] + sums[b, 8:12]
            block = pool_ref[b]
            pull = total - coordinates(block, centre) * total[3:4]
            for c in range(3):
                velocity_new = velocity_ref[c, row, :] + timestep * pull[c : c + 1]
                resident_ref[c, row, :] = block[c : c + 1, :] + timestep * velocity_new
                resident_ref[4 + c, row, :] = velocity_new
            resident_ref[3, row, :] = block[3:4, :]

    outbox_ref[...] = jnp.zeros_like(outbox_ref)
    for g in range(used.shape[0]):
        used[g] = 0
    for m in range(departures_ref.shape[0]):
        d = departures_ref[m]
        owner = owners_ref[m]
        slot = used[owner]
        used[owner] = slot + 1
        for c in range(resident_ref.shape[0]):
            outbox_ref[owner * slot_total + slot, c : c + 1, :] = resident_ref[c, pl.ds(d, 1), :]
            resident_ref[c, pl.ds(d, 1), :] = jnp.zeros((1, span), jnp.float32)


def on_device(bodies, velocity, select, pair_target, pair_source, counts, departures, owners):
    own_blocks = bodies.shape[0]
    span = bodies.shape[2]
    smem = pl.BlockSpec(memory_space=pltpu.SMEM)
    vmem = pl.BlockSpec(memory_space=pltpu.VMEM)
    steps = [
        (axis, 2**bit)
        for axis in ("gx", "gy", "gz")
        for bit in range(lax.axis_size(axis).bit_length() - 1)
    ]
    send_count = select.shape[2]
    slab = pltpu.VMEM((len(steps), send_count, 4, span), jnp.float32)
    slots = pair_target.shape[1]
    plan = early_groups(steps, slots // early_unroll)
    early = sum(plan) * early_unroll
    pool, early_sums, order = pl.pallas_call(
        functools.partial(exchange_kernel, steps, plan),
        out_shape=(
            jax.ShapeDtypeStruct((own_blocks + len(steps) * send_count, 4, span), jnp.float32),
            jax.ShapeDtypeStruct((own_blocks, 4, span), jnp.float32),
            jax.ShapeDtypeStruct((8, slots), jnp.int32),
        ),
        in_specs=[smem, smem, vmem, vmem, vmem],
        out_specs=(vmem, vmem, vmem),
        scratch_shapes=[
            slab,
            slab,
            pltpu.VMEM((own_blocks, span, 64), jnp.bfloat16),
            pltpu.VMEM((own_blocks, 16, span), jnp.bfloat16),
            pltpu.VMEM((own_blocks, 64, span), jnp.bfloat16),
            pltpu.VMEM((early, 8, span), jnp.float32),
            pltpu.SMEM((8, slots), jnp.int32),
            pltpu.SemaphoreType.DMA((len(steps),)),
            pltpu.SemaphoreType.DMA((len(steps),)),
            pltpu.SemaphoreType.DMA,
        ],
        compiler_params=pltpu.CompilerParams(
            collective_id=0, has_side_effects=True, vmem_limit_bytes=32 << 20
        ),
        name="exchange",
    )(
        jnp.transpose(select, (1, 0, 2)),
        counts,
        pair_target.reshape(slots // 128, 128),
        pair_source.reshape(slots // 128, 128),
        bodies,
    )
    group_size = lax.axis_size("gz")
    move_count = departures.shape[1]
    slot_total = max(2, 2 * move_count // group_size)
    resident, outbox = pl.pallas_call(
        functools.partial(step_kernel, slot_total, early),
        out_shape=(
            jax.ShapeDtypeStruct((7, own_blocks, span), jnp.float32),
            jax.ShapeDtypeStruct((group_size * slot_total, 7, span), jnp.float32),
        ),
        in_specs=[smem] * 4 + [vmem] * 3,
        out_specs=(vmem, vmem),
        scratch_shapes=[
            pltpu.VMEM((pool.shape[0], span, 64), jnp.bfloat16),
            pltpu.VMEM((pool.shape[0], 16, span), jnp.bfloat16),
            pltpu.VMEM((own_blocks, 64, span), jnp.bfloat16),
            pltpu.VMEM((own_blocks + 1, 16, span), jnp.float32),
            pltpu.SMEM((group_size,), jnp.int32),
        ],
        compiler_params=pltpu.CompilerParams(vmem_limit_bytes=48 << 20),
        name="gravity",
    )(
        order,
        counts,
        departures[0],
        owners[:, 0],
        pool,
        early_sums,
        jnp.transpose(velocity, (1, 0, 2)),
    )
    arrived = lax.all_to_all(
        outbox.reshape(group_size, slot_total, 7, span), "gz", split_axis=0, concat_axis=0, tiled=True
    )
    return jnp.transpose(resident, (1, 0, 2)), arrived.reshape(group_size * slot_total, 7, span)


def solution(mesh):
    everywhere = ("gx", "gy", "gz")
    cube = P(everywhere, None, None)
    flat = P(everywhere, None)
    return jax.shard_map(
        on_device,
        mesh=mesh,
        in_specs=(cube, cube, cube, flat, flat, P(everywhere), flat, flat),
        out_specs=(cube, cube),
        check_vma=False,
    )
```

```python
import functools
import math

import jax
import jax.numpy as jnp
from jax import lax
from jax.experimental import pallas as pl
from jax.experimental.pallas import tpu as pltpu
from jax.sharding import PartitionSpec as P

soften = 0.01
timestep = 0.25
deepest_unroll = 64
coarse = 2.0**14.5


def split(values):
    high = values.astype(jnp.bfloat16).astype(jnp.float32)
    rest = values - high
    middle = rest.astype(jnp.bfloat16).astype(jnp.float32)
    return high, middle, rest - middle


def frame_of(own_ref):
    lowest = jnp.min(own_ref[...], axis=0)
    highest = jnp.max(own_ref[...], axis=0)
    lowest = jnp.min(lowest, axis=1, keepdims=True)
    highest = jnp.max(highest, axis=1, keepdims=True)
    place = lax.broadcasted_iota(jnp.int32, lowest.shape, 0) < 3
    centre = jnp.where(place, 0.5 * lowest + 0.5 * highest, 0.0)
    reach = jnp.where(place, 0.5 * highest - 0.5 * lowest, 0.0)
    reach = jnp.max(reach, axis=0, keepdims=True)
    return centre, reach * coarse


def coordinates(block, centre):
    place = lax.broadcasted_iota(jnp.int32, block.shape, 0) < 3
    return jnp.where(place, block - centre, 0.0)


def pieces_of(x, grid, extra):
    coarse_x = (x + grid) - grid
    fine_x = x - coarse_x
    g1 = coarse_x.astype(jnp.bfloat16).astype(jnp.float32)
    g2 = coarse_x - g1
    f1 = fine_x.astype(jnp.bfloat16).astype(jnp.float32)
    f2 = fine_x - f1
    norm = jnp.sum(coarse_x * coarse_x, axis=0, keepdims=True)
    rest = jnp.sum(fine_x * (2.0 * coarse_x + fine_x), axis=0, keepdims=True) + extra
    return (g1, g2, f1, f2), (*split(norm), *split(rest))


meetings = ((0, 0), (0, 1), (1, 0), (1, 1), (0, 2), (2, 0), (1, 2), (2, 1), (0, 3), (3, 0), (1, 3), (3, 1), (2, 2), (2, 3), (3, 2))


def rows_of(pieces, norms, source):
    place = lax.broadcasted_iota(jnp.int32, pieces[0].shape, 0) < 3
    one = jnp.ones_like(norms[0])
    rows = []
    for n, (from_source, from_target) in enumerate(meetings):
        if n >= 2 * len(norms):
            fill = jnp.zeros_like(one)
        elif (n % 2 == 0) == source:
            fill = norms[n // 2]
        else:
            fill = one
        mine = pieces[from_source] if source else -2.0 * pieces[from_target]
        rows.append(jnp.where(place, mine, fill))
    rows.append(jnp.zeros_like(rows[0]))
    return jnp.concatenate(rows, axis=0)


def source_features(block, centre, grid):
    x = coordinates(block, centre)
    features = rows_of(*pieces_of(x, grid, 0.0), True).T.astype(jnp.bfloat16)
    mass = block[3:4]
    place = lax.broadcasted_iota(jnp.int32, block.shape, 0) < 3
    pulls = split(jnp.where(place, x * mass, mass))
    pulls = jnp.concatenate([*pulls, jnp.zeros_like(x)], axis=0).astype(jnp.bfloat16)
    return features, pulls


def target_features(block, centre, grid):
    x = coordinates(block, centre)
    return rows_of(*pieces_of(x, grid, soften), False).astype(jnp.bfloat16)


def pair_pull(source, target, pulls):
    distance = jnp.dot(source, target, preferred_element_type=jnp.float32)
    inverse = lax.rsqrt(jnp.maximum(distance, soften))
    w = inverse * inverse * inverse
    high = w.astype(jnp.bfloat16)
    low = (w - high.astype(jnp.float32)).astype(jnp.bfloat16)
    return jnp.dot(
        jnp.concatenate([pulls, pulls], axis=1),
        jnp.concatenate([high, low], axis=0),
        preferred_element_type=jnp.float32,
    )


def running_count(chosen):
    rows, lanes = chosen.shape
    before = lax.broadcasted_iota(jnp.int32, (lanes, lanes), 0) <= lax.broadcasted_iota(jnp.int32, (lanes, lanes), 1)
    running = jnp.dot(
        jnp.where(chosen, 1.0, 0.0).astype(jnp.bfloat16),
        jnp.where(before, 1.0, 0.0).astype(jnp.bfloat16),
        preferred_element_type=jnp.float32,
    )
    ends = running[:, lanes - 1 : lanes]
    earlier = lax.broadcasted_iota(jnp.int32, (rows, rows), 1) < lax.broadcasted_iota(jnp.int32, (rows, rows), 0)
    offsets = jnp.dot(
        jnp.where(earlier, 1.0, 0.0).astype(jnp.bfloat16),
        jnp.broadcast_to(ends, (rows, lanes)).astype(jnp.bfloat16),
        preferred_element_type=jnp.float32,
    )
    return running + offsets, jnp.sum(ends, axis=0, keepdims=True)


def order_pairs(pair_targets, pair_sources, count, departures, own_blocks):
    rows, lanes = pair_targets.shape
    total = rows * lanes
    place = lanes * lax.broadcasted_iota(jnp.int32, (rows, lanes), 0) + lax.broadcasted_iota(jnp.int32, (rows, lanes), 1)
    live = place < count
    own = live & (pair_sources < own_blocks)
    leaves = pair_targets == departures[0]
    for d in departures[1:]:
        leaves = leaves | (pair_targets == d)
    leaves = live & leaves & ~own
    own_count, own_total = running_count(own)
    leave_count, leave_total = running_count(leaves)
    slot = jnp.where(
        own,
        own_count - 1.0,
        jnp.where(
            leaves,
            own_total + leave_count - 1.0,
            own_total + leave_total + place.astype(jnp.float32) - own_count - leave_count,
        ),
    ).T
    digits = []
    for values in (pair_targets, pair_sources):
        digits += [(values // 128).astype(jnp.float32), (values % 128).astype(jnp.float32)]
    moved = jnp.zeros((8, total), jnp.float32)
    lane = lax.broadcasted_iota(jnp.int32, (lanes, total), 1).astype(jnp.float32)
    for r in range(rows):
        values = jnp.concatenate([d[r : r + 1] for d in digits] + [jnp.zeros((4, lanes), jnp.float32)], axis=0)
        here = jnp.where(slot[:, r : r + 1] == lane, 1.0, 0.0).astype(jnp.bfloat16)
        moved = moved + jnp.dot(values.astype(jnp.bfloat16), here, preferred_element_type=jnp.float32)
    targets = 128.0 * moved[0:1] + moved[1:2]
    sources = 128.0 * moved[2:3] + moved[3:4]
    return targets, sources, own_total, leave_total


def early_groups(steps, limit):
    plan = []
    for k, (axis, stride) in enumerate(steps):
        groups = 0 if (axis, stride) == ("gz", 1) else 1 if k == 0 else 2
        plan.append(min(groups, limit - sum(plan)))
    return plan


def exchange_kernel(
    steps,
    plan,
    unroll,
    move_count,
    table_ref,
    scalars_ref,
    count_ref,
    bodies_ref,
    pool_ref,
    sums_ref,
    order_ref,
    sources,
    pulls,
    targets,
    outgoing,
    arriving,
    parts,
    order,
    send_sem,
    recv_sem,
    order_sem,
):
    own_blocks = bodies_ref.shape[0]
    pair_rows = order_ref.shape[1] // table_ref.shape[1]
    send_count = outgoing.shape[1]
    partners = []
    for axis, stride in steps:
        me = lax.axis_index(axis)
        side = lax.rem(me // stride, 2)
        partners.append({axis: me + (1 - 2 * side) * stride})
    barrier = pltpu.get_barrier_semaphore()
    for partner in partners:
        pl.semaphore_signal(
            barrier, inc=1, device_id=partner, device_id_type=pl.DeviceIdType.MESH
        )
    pool_ref[0:own_blocks] = bodies_ref[...]
    centre, grid = frame_of(bodies_ref)
    batch = math.gcd(own_blocks, 12)

    @pl.loop(0, own_blocks // batch)
    def _(group):
        for b in [group * batch + u for u in range(batch)]:
            sources[b], pulls[b] = source_features(bodies_ref[b], centre, grid)
            targets[b] = target_features(bodies_ref[b], centre, grid)

    copies = [
        pltpu.make_async_remote_copy(
            src_ref=outgoing.at[k],
            dst_ref=arriving.at[k],
            send_sem=send_sem.at[k],
            recv_sem=recv_sem.at[k],
            device_id=partner,
            device_id_type=pl.DeviceIdType.MESH,
        )
        for k, partner in enumerate(partners)
    ]

    def send(k):
        for j in range(send_count):
            outgoing[k, j] = pool_ref[scalars_ref[2 * pair_rows + k, j]]
        copies[k].start()

    def receive(k):
        copies[k].wait_recv()
        base = own_blocks + k * send_count
        pool_ref[base : base + send_count] = arriving[k]

    def prepare(k):
        half = math.gcd(send_count, 8)

        @pl.loop(0, send_count // half)
        def _(group):
            for b in [own_blocks + k * send_count + group * half + u for u in range(half)]:
                sources[b], pulls[b] = source_features(pool_ref[b], centre, grid)

    pl.semaphore_wait(barrier, len(partners))
    send(0)
    departures = [scalars_ref[2 * pair_rows + len(steps), m] for m in range(move_count)]
    row_t, row_s, own_total, leave_total = order_pairs(
        table_ref[0:pair_rows], table_ref[pair_rows : 2 * pair_rows], count_ref[0], departures, own_blocks
    )
    slots = row_t.shape[1]
    table = [row_t, row_s, jnp.broadcast_to(own_total, row_t.shape), jnp.broadcast_to(leave_total, row_t.shape)]
    table = jnp.concatenate([*table, jnp.zeros((4, slots), jnp.float32)], axis=0)
    order_ref[...] = table.astype(jnp.int32)
    into_order = pltpu.make_async_copy(order_ref, order, order_sem)
    into_order.start()
    into_order.wait()

    @pl.loop(0, sum(plan))
    def _(group):
        for k in range(1, len(partners)):

            @pl.when(group == sum(plan[:k]))
            def _():
                receive(k - 1)
                send(k)
                prepare(k - 1)

        for u in range(unroll):
            p = group * unroll + u
            t = jnp.clip(order[0, p], 0, own_blocks - 1)
            s = jnp.clip(order[1, p], 0, own_blocks - 1)
            pull = pair_pull(sources[s], targets[t], pulls[s])
            parts[p] = pull[0:8] + pull[8:16]

    for k in range(1, len(partners)):
        if sum(plan[:k]) >= sum(plan):
            receive(k - 1)
            send(k)
            prepare(k - 1)
    early = parts.shape[0]
    members = lax.broadcasted_iota(jnp.int32, (-(-own_blocks // 16) * 16, early), 0)
    spot = lax.broadcasted_iota(jnp.int32, members.shape, 1).astype(jnp.float32)
    chosen = (members == order_ref[0:1, 0:early]) & (spot < own_total)
    chosen = jnp.where(chosen, 1.0, 0.0).astype(jnp.bfloat16)
    for c in range(4):
        total = jnp.zeros((members.shape[0], parts.shape[2]), jnp.float32)
        for piece in split(parts[:, c, :] + parts[:, c + 4, :]):
            total = total + jnp.dot(chosen, piece.astype(jnp.bfloat16), preferred_element_type=jnp.float32)
        sums_ref[:, c, :] = total[0:own_blocks]
    receive(len(partners) - 1)
    prepare(len(partners) - 1)
    for copy in copies:
        copy.wait_send()


def pull_loop(first, last, order_ref, sources, targets, pulls, sums, unroll):
    slots = order_ref.shape[1]
    nowhere = sums.shape[0] - 1

    @pl.loop(0, (last - first + unroll - 1) // unroll)
    def _(group):
        for u in range(unroll):
            p = first + group * unroll + u
            live = p < last
            p = jnp.minimum(p, slots - 1)
            t = order_ref[0, p]
            s = order_ref[1, p]
            where = jnp.where(live, t, nowhere)
            sums[where] += pair_pull(sources[s], targets[t], pulls[s])


def update(b, centre, pool_ref, sums, velocity_ref):
    total = sums[b, 0:4] + sums[b, 4:8] + sums[b, 8:12]
    block = pool_ref[b]
    pull = total - coordinates(block, centre) * total[3:4]
    places, velocities = [], []
    for c in range(3):
        velocity_new = velocity_ref[c, pl.ds(b, 1), :] + timestep * pull[c : c + 1]
        velocities.append(velocity_new)
        places.append(block[c : c + 1, :] + timestep * velocity_new)
    return [*places, block[3:4, :], *velocities]


def leaving_kernel(
    unroll,
    early,
    move_row,
    move_count,
    order_ref,
    scalars_ref,
    pool_ref,
    early_sums_ref,
    velocity_hbm,
    sources,
    pulls,
    targets,
    sums,
    *rest,
):
    outboxes, (boxes, used, velocity_ref, load_sem) = rest[:-4], rest[-4:]
    own_blocks = early_sums_ref.shape[0]
    span = pool_ref.shape[2]
    load = pltpu.make_async_copy(velocity_hbm, velocity_ref, load_sem)
    load.start()
    own_total = order_ref[2, 0]
    centre, _ = frame_of(pool_ref.at[pl.ds(0, own_blocks)])
    sums[0:own_blocks, 0:4] = early_sums_ref[...]
    sums[0:own_blocks, 4:16] = jnp.zeros((own_blocks, 12, span), jnp.float32)
    sums[own_blocks] = jnp.zeros(sums.shape[1:], jnp.float32)
    boxes[...] = jnp.zeros_like(boxes)
    for g in range(used.shape[0]):
        used[g] = 0
    pull_loop(
        jnp.minimum(own_total, early), own_total + order_ref[3, 0], order_ref, sources, targets, pulls, sums, unroll
    )
    load.wait()
    me = lax.axis_index("gz")
    for m in range(move_count):
        owner = scalars_ref[move_row + 1, m]
        slot = used[owner]
        used[owner] = slot + 1
        box = jnp.bitwise_xor(owner, me)
        for c, row in enumerate(update(scalars_ref[move_row, m], centre, pool_ref, sums, velocity_ref)):
            boxes[box, slot, c : c + 1, :] = row
    for g, outbox in enumerate(outboxes):
        outbox[...] = boxes[g]


def staying_kernel(
    unroll,
    move_row,
    move_count,
    order_ref,
    scalars_ref,
    count_ref,
    pool_ref,
    sums_ref,
    velocity_hbm,
    sources,
    pulls,
    targets,
    resident_ref,
    sums,
    velocity_ref,
    load_sem,
):
    own_blocks = sums_ref.shape[0] - 1
    span = pool_ref.shape[2]
    load = pltpu.make_async_copy(velocity_hbm, velocity_ref, load_sem)
    load.start()
    centre, _ = frame_of(pool_ref.at[pl.ds(0, own_blocks)])
    sums[...] = sums_ref[...]
    pull_loop(order_ref[2, 0] + order_ref[3, 0], count_ref[0], order_ref, sources, targets, pulls, sums, unroll)
    load.wait()
    batch = math.gcd(own_blocks, 12)

    @pl.loop(0, own_blocks // batch)
    def _(group):
        for b in [group * batch + u for u in range(batch)]:
            for c, row in enumerate(update(b, centre, pool_ref, sums, velocity_ref)):
                resident_ref[c, pl.ds(b, 1), :] = row

    for m in range(move_count):
        for c in range(resident_ref.shape[0]):
            resident_ref[c, pl.ds(scalars_ref[move_row, m], 1), :] = jnp.zeros((1, span), jnp.float32)


def inbox_kernel(*refs):
    boxes, moved_ref = refs[:-1], refs[-1]
    me = lax.axis_index("gz")
    slot_total = boxes[0].shape[0]
    for g, box in enumerate(boxes):
        sender = jnp.bitwise_xor(me, g)
        for slot in range(slot_total):
            for c in range(moved_ref.shape[0]):
                moved_ref[c, pl.ds(sender * slot_total + slot, 1), :] = box[slot, c : c + 1, :]


def on_device(bodies, velocity, select, pair_target, pair_source, counts, departures, owners):
    own_blocks = bodies.shape[0]
    span = bodies.shape[2]
    smem = pl.BlockSpec(memory_space=pltpu.SMEM)
    vmem = pl.BlockSpec(memory_space=pltpu.VMEM)
    steps = [
        (axis, 2**bit)
        for axis in ("gx", "gy", "gz")
        for bit in range(lax.axis_size(axis).bit_length() - 1)
    ]
    send_count = select.shape[2]
    slab = pltpu.VMEM((len(steps), send_count, 4, span), jnp.float32)
    slots = pair_target.shape[1]
    unroll = math.gcd(slots, deepest_unroll)
    plan = early_groups(steps, slots // unroll)
    early = sum(plan) * unroll
    pool_size = own_blocks + len(steps) * send_count
    move_count = departures.shape[1]
    hbm = pl.BlockSpec(memory_space=pltpu.MemorySpace.HBM)
    pair_rows = slots // 128
    move_row = 2 * pair_rows + len(steps)
    table = jnp.concatenate(
        [
            pair_target.reshape(pair_rows, 128),
            pair_source.reshape(pair_rows, 128),
            jnp.pad(select[0], ((0, 0), (0, 128 - send_count))),
            jnp.pad(departures, ((0, 0), (0, 128 - move_count))),
            jnp.pad(jnp.transpose(owners, (1, 0)), ((0, -(move_row + 2) % 8), (0, 128 - move_count))),
        ],
        axis=0,
    )
    velocity = jnp.transpose(velocity, (1, 0, 2))
    pool, early_sums, order, sources, pulls, targets = pl.pallas_call(
        functools.partial(exchange_kernel, steps, plan, unroll, move_count),
        out_shape=(
            jax.ShapeDtypeStruct((pool_size, 4, span), jnp.float32),
            jax.ShapeDtypeStruct((own_blocks, 4, span), jnp.float32),
            jax.ShapeDtypeStruct((8, slots), jnp.int32),
            jax.ShapeDtypeStruct((pool_size, span, 64), jnp.bfloat16),
            jax.ShapeDtypeStruct((pool_size, 16, span), jnp.bfloat16),
            jax.ShapeDtypeStruct((own_blocks, 64, span), jnp.bfloat16),
        ),
        in_specs=[vmem, smem, smem, vmem],
        out_specs=(vmem,) * 6,
        scratch_shapes=[
            slab,
            slab,
            pltpu.VMEM((early, 8, span), jnp.float32),
            pltpu.SMEM((8, slots), jnp.int32),
            pltpu.SemaphoreType.DMA((len(steps),)),
            pltpu.SemaphoreType.DMA((len(steps),)),
            pltpu.SemaphoreType.DMA,
        ],
        compiler_params=pltpu.CompilerParams(
            collective_id=0, has_side_effects=True, vmem_limit_bytes=32 << 20
        ),
        name="exchange",
    )(table, table, counts, bodies)
    group_size = lax.axis_size("gz")
    slot_total = max(2, 2 * move_count // group_size)
    work = pl.CostEstimate(flops=20 * slots // 4 * span * span, bytes_accessed=1 << 20, transcendentals=0)
    box = jax.ShapeDtypeStruct((slot_total, 7, span), jnp.float32)
    sums, *outboxes = pl.pallas_call(
        functools.partial(leaving_kernel, unroll, early, move_row, move_count),
        out_shape=(jax.ShapeDtypeStruct((own_blocks + 1, 16, span), jnp.float32),) + (box,) * group_size,
        in_specs=[smem, smem, vmem, vmem, hbm, vmem, vmem, vmem],
        out_specs=(vmem,) * (1 + group_size),
        scratch_shapes=[
            pltpu.VMEM((group_size, slot_total, 7, span), jnp.float32),
            pltpu.SMEM((group_size,), jnp.int32),
            pltpu.VMEM((3, own_blocks, span), jnp.float32),
            pltpu.SemaphoreType.DMA,
        ],
        compiler_params=pltpu.CompilerParams(vmem_limit_bytes=24 << 20),
        cost_estimate=work,
        name="leaving",
    )(order, table, pool, early_sums, velocity, sources, pulls, targets)
    inboxes = [outboxes[0]]
    for g in range(1, group_size):
        pairs = [(i, i ^ g) for i in range(group_size)]
        inboxes.append(lax.ppermute(outboxes[g], "gz", pairs))
    resident = pl.pallas_call(
        functools.partial(staying_kernel, unroll, move_row, move_count),
        out_shape=jax.ShapeDtypeStruct((7, own_blocks, span), jnp.float32),
        in_specs=[smem, smem, smem, vmem, vmem, hbm, vmem, vmem, vmem],
        out_specs=vmem,
        scratch_shapes=[
            pltpu.VMEM((own_blocks + 1, 16, span), jnp.float32),
            pltpu.VMEM((3, own_blocks, span), jnp.float32),
            pltpu.SemaphoreType.DMA,
        ],
        compiler_params=pltpu.CompilerParams(vmem_limit_bytes=24 << 20),
        cost_estimate=work,
        name="staying",
    )(order, table, counts, pool, sums, velocity, sources, pulls, targets)
    moved = pl.pallas_call(
        inbox_kernel,
        out_shape=jax.ShapeDtypeStruct((7, group_size * slot_total, span), jnp.float32),
        in_specs=[vmem] * group_size,
        out_specs=vmem,
        compiler_params=pltpu.CompilerParams(vmem_limit_bytes=16 << 20),
        name="inbox",
    )(*inboxes)
    return jnp.transpose(resident, (1, 0, 2)), jnp.transpose(moved, (1, 0, 2))


def solution(mesh):
    everywhere = ("gx", "gy", "gz")
    cube = P(everywhere, None, None)
    flat = P(everywhere, None)
    return jax.shard_map(
        on_device,
        mesh=mesh,
        in_specs=(cube, cube, cube, flat, flat, P(everywhere), flat, flat),
        out_specs=(cube, cube),
        check_vma=False,
    )
```

```python
import functools
import math

import jax
import jax.numpy as jnp
from jax import lax
from jax.experimental import pallas as pl
from jax.experimental.pallas import tpu as pltpu
from jax.sharding import PartitionSpec as P

soften = 0.01
timestep = 0.25
deepest_unroll = 64
moves_radix = 1 << 16
coarse = 2.0**14.5


def split(values):
    high = values.astype(jnp.bfloat16).astype(jnp.float32)
    rest = values - high
    middle = rest.astype(jnp.bfloat16).astype(jnp.float32)
    return high, middle, rest - middle


def frame_of(own_ref):
    lowest = jnp.min(own_ref[...], axis=0)
    highest = jnp.max(own_ref[...], axis=0)
    lowest = jnp.min(lowest, axis=1, keepdims=True)
    highest = jnp.max(highest, axis=1, keepdims=True)
    place = lax.broadcasted_iota(jnp.int32, lowest.shape, 0) < 3
    centre = jnp.where(place, 0.5 * lowest + 0.5 * highest, 0.0)
    reach = jnp.where(place, 0.5 * highest - 0.5 * lowest, 0.0)
    reach = jnp.max(reach, axis=0, keepdims=True)
    return centre, reach * coarse


def coordinates(block, centre):
    place = lax.broadcasted_iota(jnp.int32, block.shape, 0) < 3
    return jnp.where(place, block - centre, 0.0)


def pieces_of(x, grid, extra):
    coarse_x = (x + grid) - grid
    fine_x = x - coarse_x
    g1 = coarse_x.astype(jnp.bfloat16).astype(jnp.float32)
    g2 = coarse_x - g1
    f1 = fine_x.astype(jnp.bfloat16).astype(jnp.float32)
    f2 = fine_x - f1
    norm = jnp.sum(coarse_x * coarse_x, axis=0, keepdims=True)
    rest = jnp.sum(fine_x * (2.0 * coarse_x + fine_x), axis=0, keepdims=True) + extra
    return (g1, g2, f1, f2), (*split(norm), *split(rest))


meetings = ((0, 0), (0, 1), (1, 0), (1, 1), (0, 2), (2, 0), (1, 2), (2, 1), (0, 3), (3, 0), (1, 3), (3, 1), (2, 2), (2, 3), (3, 2))


def rows_of(pieces, norms, source):
    place = lax.broadcasted_iota(jnp.int32, pieces[0].shape, 0) < 3
    one = jnp.ones_like(norms[0])
    rows = []
    for n, (from_source, from_target) in enumerate(meetings):
        if n >= 2 * len(norms):
            fill = jnp.zeros_like(one)
        elif (n % 2 == 0) == source:
            fill = norms[n // 2]
        else:
            fill = one
        mine = pieces[from_source] if source else -2.0 * pieces[from_target]
        rows.append(jnp.where(place, mine, fill))
    rows.append(jnp.zeros_like(rows[0]))
    return jnp.concatenate(rows, axis=0)


def source_features(block, centre, grid):
    x = coordinates(block, centre)
    features = rows_of(*pieces_of(x, grid, 0.0), True).T.astype(jnp.bfloat16)
    mass = block[3:4]
    place = lax.broadcasted_iota(jnp.int32, block.shape, 0) < 3
    pulls = split(jnp.where(place, x * mass, mass))
    pulls = jnp.concatenate([*pulls, jnp.zeros_like(x)], axis=0).astype(jnp.bfloat16)
    return features, pulls


def target_features(block, centre, grid):
    x = coordinates(block, centre)
    return rows_of(*pieces_of(x, grid, soften), False).astype(jnp.bfloat16)


def pair_pull(source, target, pulls):
    distance = jnp.dot(source, target, preferred_element_type=jnp.float32)
    inverse = lax.rsqrt(jnp.maximum(distance, soften))
    w = inverse * inverse * inverse
    high = w.astype(jnp.bfloat16)
    low = (w - high.astype(jnp.float32)).astype(jnp.bfloat16)
    return jnp.dot(
        jnp.concatenate([pulls, pulls], axis=1),
        jnp.concatenate([high, low], axis=0),
        preferred_element_type=jnp.float32,
    )


def running_count(chosen):
    rows, lanes = chosen.shape
    before = lax.broadcasted_iota(jnp.int32, (lanes, lanes), 0) <= lax.broadcasted_iota(jnp.int32, (lanes, lanes), 1)
    running = jnp.dot(
        jnp.where(chosen, 1.0, 0.0).astype(jnp.bfloat16),
        jnp.where(before, 1.0, 0.0).astype(jnp.bfloat16),
        preferred_element_type=jnp.float32,
    )
    ends = running[:, lanes - 1 : lanes]
    earlier = lax.broadcasted_iota(jnp.int32, (rows, rows), 1) < lax.broadcasted_iota(jnp.int32, (rows, rows), 0)
    offsets = jnp.dot(
        jnp.where(earlier, 1.0, 0.0).astype(jnp.bfloat16),
        jnp.broadcast_to(ends, (rows, lanes)).astype(jnp.bfloat16),
        preferred_element_type=jnp.float32,
    )
    return running + offsets, jnp.sum(ends, axis=0, keepdims=True)


def order_pairs(coded, radix, departures, own_blocks):
    rows, lanes = coded.shape
    total = rows * lanes
    place = lanes * lax.broadcasted_iota(jnp.int32, (rows, lanes), 0) + lax.broadcasted_iota(jnp.int32, (rows, lanes), 1)
    live = coded >= 0
    coded = jnp.maximum(coded, 0)
    pair_targets = coded // radix
    pair_sources = coded % radix
    own = live & (pair_sources < own_blocks)
    leaves = pair_targets == departures[0]
    for d in departures[1:]:
        leaves = leaves | (pair_targets == d)
    leaves = live & leaves & ~own
    own_count, own_total = running_count(own)
    leave_count, leave_total = running_count(leaves)
    slot = jnp.where(
        own,
        own_count - 1.0,
        jnp.where(
            leaves,
            own_total + leave_count - 1.0,
            own_total + leave_total + place.astype(jnp.float32) - own_count - leave_count,
        ),
    ).T
    digits = []
    for values in (pair_targets, pair_sources):
        digits += [(values // 128).astype(jnp.float32), (values % 128).astype(jnp.float32)]
    moved = jnp.zeros((8, total), jnp.float32)
    lane = lax.broadcasted_iota(jnp.int32, (lanes, total), 1).astype(jnp.float32)
    for r in range(rows):
        values = jnp.concatenate([d[r : r + 1] for d in digits] + [jnp.zeros((4, lanes), jnp.float32)], axis=0)
        here = jnp.where(slot[:, r : r + 1] == lane, 1.0, 0.0).astype(jnp.bfloat16)
        moved = moved + jnp.dot(values.astype(jnp.bfloat16), here, preferred_element_type=jnp.float32)
    targets = 128.0 * moved[0:1] + moved[1:2]
    sources = 128.0 * moved[2:3] + moved[3:4]
    live_total = jnp.sum(jnp.where(live, 1.0, 0.0), axis=1, keepdims=True)
    return targets, sources, own_total, leave_total, jnp.sum(live_total, axis=0, keepdims=True)


def early_groups(steps, limit):
    plan = []
    for k, (axis, stride) in enumerate(steps):
        groups = 0 if (axis, stride) == ("gz", 1) else 1 if k == 0 else 2
        plan.append(min(groups, limit - sum(plan)))
    return plan


def exchange_kernel(
    steps,
    plan,
    unroll,
    radix,
    coded_ref,
    select_vmem,
    moves_vmem,
    bodies_ref,
    pool_ref,
    sums_ref,
    order_ref,
    sources,
    pulls,
    targets,
    outgoing,
    arriving,
    parts,
    order,
    select_ref,
    moves_ref,
    send_sem,
    recv_sem,
    load_sem,
):
    own_blocks = bodies_ref.shape[0]
    send_count = outgoing.shape[1]
    partners = []
    for axis, stride in steps:
        me = lax.axis_index(axis)
        side = lax.rem(me // stride, 2)
        partners.append({axis: me + (1 - 2 * side) * stride})
    barrier = pltpu.get_barrier_semaphore()
    for partner in partners:
        pl.semaphore_signal(
            barrier, inc=1, device_id=partner, device_id_type=pl.DeviceIdType.MESH
        )
    load_select = pltpu.make_async_copy(select_vmem, select_ref, load_sem.at[0])
    load_moves = pltpu.make_async_copy(moves_vmem, moves_ref, load_sem.at[1])
    load_select.start()
    load_moves.start()
    pool_ref[0:own_blocks] = bodies_ref[...]
    centre, grid = frame_of(bodies_ref)
    batch = math.gcd(own_blocks, 12)

    @pl.loop(0, own_blocks // batch)
    def _(group):
        for b in [group * batch + u for u in range(batch)]:
            sources[b], pulls[b] = source_features(bodies_ref[b], centre, grid)
            targets[b] = target_features(bodies_ref[b], centre, grid)

    copies = [
        pltpu.make_async_remote_copy(
            src_ref=outgoing.at[k],
            dst_ref=arriving.at[k],
            send_sem=send_sem.at[k],
            recv_sem=recv_sem.at[k],
            device_id=partner,
            device_id_type=pl.DeviceIdType.MESH,
        )
        for k, partner in enumerate(partners)
    ]

    def send(k):
        for j in range(send_count):
            outgoing[k, j] = pool_ref[select_ref[k, 0, j]]
        copies[k].start()

    def receive(k):
        copies[k].wait_recv()
        base = own_blocks + k * send_count
        pool_ref[base : base + send_count] = arriving[k]

    def prepare(k):
        half = math.gcd(send_count, 8)

        @pl.loop(0, send_count // half)
        def _(group):
            for b in [own_blocks + k * send_count + group * half + u for u in range(half)]:
                sources[b], pulls[b] = source_features(pool_ref[b], centre, grid)

    load_select.wait()
    load_moves.wait()
    pl.semaphore_wait(barrier, len(partners))
    send(0)
    departures = [moves_ref[0, m] // moves_radix for m in range(moves_ref.shape[1])]
    row_t, row_s, *totals = order_pairs(coded_ref[...], radix, departures, own_blocks)
    own_total = totals[0]
    slots = row_t.shape[1]
    table = [row_t, row_s, *[jnp.broadcast_to(total, row_t.shape) for total in totals]]
    table = jnp.concatenate([*table, jnp.zeros((8 - len(table), slots), jnp.float32)], axis=0)
    order_ref[...] = table.astype(jnp.int32)
    into_order = pltpu.make_async_copy(order_ref, order, load_sem.at[0])
    into_order.start()
    into_order.wait()

    @pl.loop(0, sum(plan))
    def _(group):
        for k in range(1, len(partners)):

            @pl.when(group == sum(plan[:k]))
            def _():
                receive(k - 1)
                send(k)
                prepare(k - 1)

        for u in range(unroll):
            p = group * unroll + u
            t = jnp.clip(order[0, p], 0, own_blocks - 1)
            s = jnp.clip(order[1, p], 0, own_blocks - 1)
            pull = pair_pull(sources[s], targets[t], pulls[s])
            parts[p] = pull[0:8] + pull[8:16]

    for k in range(1, len(partners)):
        if sum(plan[:k]) >= sum(plan):
            receive(k - 1)
            send(k)
            prepare(k - 1)
    early = parts.shape[0]
    members = lax.broadcasted_iota(jnp.int32, (-(-own_blocks // 16) * 16, early), 0)
    spot = lax.broadcasted_iota(jnp.int32, members.shape, 1).astype(jnp.float32)
    chosen = (members == order_ref[0:1, 0:early]) & (spot < own_total)
    chosen = jnp.where(chosen, 1.0, 0.0).astype(jnp.bfloat16)
    for c in range(4):
        total = jnp.zeros((members.shape[0], parts.shape[2]), jnp.float32)
        for piece in split(parts[:, c, :] + parts[:, c + 4, :]):
            total = total + jnp.dot(chosen, piece.astype(jnp.bfloat16), preferred_element_type=jnp.float32)
        sums_ref[:, c, :] = total[0:own_blocks]
    receive(len(partners) - 1)
    prepare(len(partners) - 1)
    for copy in copies:
        copy.wait_send()


def pull_loop(first, last, order_ref, sources, targets, pulls, sums, unroll):
    slots = order_ref.shape[1]
    nowhere = sums.shape[0] - 1

    @pl.loop(0, (last - first + unroll - 1) // unroll)
    def _(group):
        for u in range(unroll):
            p = first + group * unroll + u
            live = p < last
            p = jnp.minimum(p, slots - 1)
            t = order_ref[0, p]
            s = order_ref[1, p]
            where = jnp.where(live, t, nowhere)
            sums[where] += pair_pull(sources[s], targets[t], pulls[s])


def update(b, centre, pool_ref, sums, velocity_ref):
    total = sums[b, 0:4] + sums[b, 4:8] + sums[b, 8:12]
    block = pool_ref[b]
    pull = total - coordinates(block, centre) * total[3:4]
    places, velocities = [], []
    for c in range(3):
        velocity_new = velocity_ref[c, pl.ds(b, 1), :] + timestep * pull[c : c + 1]
        velocities.append(velocity_new)
        places.append(block[c : c + 1, :] + timestep * velocity_new)
    return [*places, block[3:4, :], *velocities]


def leaving_range(order_ref, early, unroll):
    first = jnp.minimum(order_ref[2, 0], early)
    groups = (order_ref[2, 0] + order_ref[3, 0] - first + unroll - 1) // unroll
    return first, jnp.minimum(first + groups * unroll, order_ref[4, 0])


def leaving_kernel(
    unroll,
    early,
    order_ref,
    moves_ref,
    pool_ref,
    early_sums_ref,
    velocity_ref,
    sources,
    pulls,
    targets,
    sums,
    *rest,
):
    outboxes, (boxes, used) = rest[:-2], rest[-2:]
    own_blocks = early_sums_ref.shape[0]
    span = pool_ref.shape[2]
    centre, _ = frame_of(pool_ref.at[pl.ds(0, own_blocks)])
    sums[0:own_blocks, 0:4] = early_sums_ref[...]
    sums[0:own_blocks, 4:16] = jnp.zeros((own_blocks, 12, span), jnp.float32)
    sums[own_blocks] = jnp.zeros(sums.shape[1:], jnp.float32)
    boxes[...] = jnp.zeros_like(boxes)
    for g in range(used.shape[0]):
        used[g] = 0
    pull_loop(*leaving_range(order_ref, early, unroll), order_ref, sources, targets, pulls, sums, unroll)
    me = lax.axis_index("gz")
    for m in range(moves_ref.shape[1]):
        owner = moves_ref[0, m] % moves_radix
        slot = used[owner]
        used[owner] = slot + 1
        box = jnp.bitwise_xor(owner, me)
        for c, row in enumerate(update(moves_ref[0, m] // moves_radix, centre, pool_ref, sums, velocity_ref)):
            boxes[box, slot, c : c + 1, :] = row
    for g, outbox in enumerate(outboxes):
        outbox[...] = boxes[g]


def staying_kernel(
    unroll,
    early,
    order_ref,
    moves_ref,
    pool_ref,
    sums_ref,
    velocity_ref,
    sources,
    pulls,
    targets,
    resident_ref,
    sums,
):
    own_blocks = sums_ref.shape[0] - 1
    span = pool_ref.shape[2]
    centre, _ = frame_of(pool_ref.at[pl.ds(0, own_blocks)])
    sums[...] = sums_ref[...]
    _, first = leaving_range(order_ref, early, unroll)
    pull_loop(first, order_ref[4, 0], order_ref, sources, targets, pulls, sums, unroll)
    batch = math.gcd(own_blocks, 12)

    @pl.loop(0, own_blocks // batch)
    def _(group):
        for b in [group * batch + u for u in range(batch)]:
            for c, row in enumerate(update(b, centre, pool_ref, sums, velocity_ref)):
                resident_ref[c, pl.ds(b, 1), :] = row

    for m in range(moves_ref.shape[1]):
        for c in range(resident_ref.shape[0]):
            resident_ref[c, pl.ds(moves_ref[0, m] // moves_radix, 1), :] = jnp.zeros((1, span), jnp.float32)


def inbox_kernel(*refs):
    boxes, moved_ref = refs[:-1], refs[-1]
    me = lax.axis_index("gz")
    slot_total = boxes[0].shape[0]
    for g, box in enumerate(boxes):
        sender = jnp.bitwise_xor(me, g)
        for slot in range(slot_total):
            for c in range(moved_ref.shape[0]):
                moved_ref[c, pl.ds(sender * slot_total + slot, 1), :] = box[slot, c : c + 1, :]


def on_device(bodies, velocity, select, pair_target, pair_source, counts, departures, owners):
    own_blocks = bodies.shape[0]
    span = bodies.shape[2]
    smem = pl.BlockSpec(memory_space=pltpu.SMEM)
    vmem = pl.BlockSpec(memory_space=pltpu.VMEM)
    steps = [
        (axis, 2**bit)
        for axis in ("gx", "gy", "gz")
        for bit in range(lax.axis_size(axis).bit_length() - 1)
    ]
    send_count = select.shape[2]
    slab = pltpu.VMEM((len(steps), send_count, 4, span), jnp.float32)
    slots = pair_target.shape[1]
    unroll = math.gcd(slots, deepest_unroll)
    plan = early_groups(steps, slots // unroll)
    early = sum(plan) * unroll
    pool_size = own_blocks + len(steps) * send_count
    move_count = departures.shape[1]
    radix = 1 << (pool_size - 1).bit_length()
    place = lax.broadcasted_iota(jnp.int32, pair_target.shape, 1)
    coded = jnp.where(place < counts[None, :], pair_target * radix + pair_source, -1).reshape(slots // 128, 128)
    moves = departures * moves_radix + jnp.transpose(owners, (1, 0))
    velocity = jnp.transpose(velocity, (1, 0, 2))
    pool, early_sums, order, sources, pulls, targets = pl.pallas_call(
        functools.partial(exchange_kernel, steps, plan, unroll, radix),
        out_shape=(
            jax.ShapeDtypeStruct((pool_size, 4, span), jnp.float32),
            jax.ShapeDtypeStruct((own_blocks, 4, span), jnp.float32),
            jax.ShapeDtypeStruct((8, slots), jnp.int32),
            jax.ShapeDtypeStruct((pool_size, span, 64), jnp.bfloat16),
            jax.ShapeDtypeStruct((pool_size, 16, span), jnp.bfloat16),
            jax.ShapeDtypeStruct((own_blocks, 64, span), jnp.bfloat16),
        ),
        in_specs=[vmem] * 4,
        out_specs=(vmem,) * 6,
        scratch_shapes=[
            slab,
            slab,
            pltpu.VMEM((early, 8, span), jnp.float32),
            pltpu.SMEM((8, slots), jnp.int32),
            pltpu.SMEM((len(steps), 1, send_count), jnp.int32),
            pltpu.SMEM((1, move_count), jnp.int32),
            pltpu.SemaphoreType.DMA((len(steps),)),
            pltpu.SemaphoreType.DMA((len(steps),)),
            pltpu.SemaphoreType.DMA((2,)),
        ],
        compiler_params=pltpu.CompilerParams(
            collective_id=0, has_side_effects=True, vmem_limit_bytes=32 << 20
        ),
        cost_estimate=pl.CostEstimate(flops=10**10, bytes_accessed=1048576, transcendentals=0),
        name="exchange",
    )(coded, jnp.transpose(select, (1, 0, 2)), moves, bodies)
    group_size = lax.axis_size("gz")
    slot_total = max(2, 2 * move_count // group_size)
    work = pl.CostEstimate(flops=20 * slots // 4 * span * span, bytes_accessed=1 << 20, transcendentals=0)
    box = jax.ShapeDtypeStruct((slot_total, 7, span), jnp.float32)
    sums, *outboxes = pl.pallas_call(
        functools.partial(leaving_kernel, unroll, early),
        out_shape=(jax.ShapeDtypeStruct((own_blocks + 1, 16, span), jnp.float32),) + (box,) * group_size,
        in_specs=[smem, smem] + [vmem] * 6,
        out_specs=(vmem,) * (1 + group_size),
        scratch_shapes=[
            pltpu.VMEM((group_size, slot_total, 7, span), jnp.float32),
            pltpu.SMEM((group_size,), jnp.int32),
        ],
        compiler_params=pltpu.CompilerParams(vmem_limit_bytes=24 << 20),
        name="leaving",
    )(order, moves, pool, early_sums, velocity, sources, pulls, targets)
    inboxes = [outboxes[0]]
    for g in range(1, group_size):
        pairs = [(i, i ^ g) for i in range(group_size)]
        inboxes.append(lax.ppermute(outboxes[g], "gz", pairs))
    resident = pl.pallas_call(
        functools.partial(staying_kernel, unroll, early),
        out_shape=jax.ShapeDtypeStruct((7, own_blocks, span), jnp.float32),
        in_specs=[smem, smem] + [vmem] * 6,
        out_specs=vmem,
        scratch_shapes=[pltpu.VMEM((own_blocks + 1, 16, span), jnp.float32)],
        compiler_params=pltpu.CompilerParams(vmem_limit_bytes=24 << 20),
        cost_estimate=work,
        name="staying",
    )(order, moves, pool, sums, velocity, sources, pulls, targets)
    moved = pl.pallas_call(
        inbox_kernel,
        out_shape=jax.ShapeDtypeStruct((7, group_size * slot_total, span), jnp.float32),
        in_specs=[vmem] * group_size,
        out_specs=vmem,
        compiler_params=pltpu.CompilerParams(vmem_limit_bytes=16 << 20),
        name="inbox",
    )(*inboxes)
    return jnp.transpose(resident, (1, 0, 2)), jnp.transpose(moved, (1, 0, 2))


def solution(mesh):
    everywhere = ("gx", "gy", "gz")
    cube = P(everywhere, None, None)
    flat = P(everywhere, None)
    return jax.shard_map(
        on_device,
        mesh=mesh,
        in_specs=(cube, cube, cube, flat, flat, P(everywhere), flat, flat),
        out_specs=(cube, cube),
        check_vma=False,
    )
```

```python
import functools
import math

import jax
import jax.numpy as jnp
from jax import lax
from jax.experimental import pallas as pl
from jax.experimental.pallas import tpu as pltpu
from jax.sharding import PartitionSpec as P

soften = 0.01
timestep = 0.25
deepest_unroll = 64
moves_radix = 1 << 16
coarse = 2.0**14.5


def split(values):
    high = values.astype(jnp.bfloat16).astype(jnp.float32)
    rest = values - high
    middle = rest.astype(jnp.bfloat16).astype(jnp.float32)
    return high, middle, rest - middle


def frame_of(own_ref):
    lowest = jnp.min(own_ref[...], axis=0)
    highest = jnp.max(own_ref[...], axis=0)
    lowest = jnp.min(lowest, axis=1, keepdims=True)
    highest = jnp.max(highest, axis=1, keepdims=True)
    place = lax.broadcasted_iota(jnp.int32, lowest.shape, 0) < 3
    centre = jnp.where(place, 0.5 * lowest + 0.5 * highest, 0.0)
    reach = jnp.where(place, 0.5 * highest - 0.5 * lowest, 0.0)
    reach = jnp.max(reach, axis=0, keepdims=True)
    return centre, reach * coarse


def coordinates(block, centre):
    place = lax.broadcasted_iota(jnp.int32, block.shape, 0) < 3
    return jnp.where(place, block - centre, 0.0)


def pieces_of(x, grid, extra):
    coarse_x = (x + grid) - grid
    fine_x = x - coarse_x
    g1 = coarse_x.astype(jnp.bfloat16).astype(jnp.float32)
    g2 = coarse_x - g1
    f1 = fine_x.astype(jnp.bfloat16).astype(jnp.float32)
    f2 = fine_x - f1
    norm = jnp.sum(coarse_x * coarse_x, axis=0, keepdims=True)
    rest = jnp.sum(fine_x * (2.0 * coarse_x + fine_x), axis=0, keepdims=True) + extra
    return (g1, g2, f1, f2), (*split(norm), *split(rest))


meetings = ((0, 0), (0, 1), (1, 0), (1, 1), (0, 2), (2, 0), (1, 2), (2, 1), (0, 3), (3, 0), (1, 3), (3, 1), (2, 2), (2, 3), (3, 2))


def rows_of(pieces, norms, source):
    place = lax.broadcasted_iota(jnp.int32, pieces[0].shape, 0) < 3
    one = jnp.ones_like(norms[0])
    rows = []
    for n, (from_source, from_target) in enumerate(meetings):
        if n >= 2 * len(norms):
            fill = jnp.zeros_like(one)
        elif (n % 2 == 0) == source:
            fill = norms[n // 2]
        else:
            fill = one
        mine = pieces[from_source] if source else -2.0 * pieces[from_target]
        rows.append(jnp.where(place, mine, fill))
    rows.append(jnp.zeros_like(rows[0]))
    return jnp.concatenate(rows, axis=0)


def source_features(block, centre, grid):
    x = coordinates(block, centre)
    features = rows_of(*pieces_of(x, grid, 0.0), True).T.astype(jnp.bfloat16)
    mass = block[3:4]
    place = lax.broadcasted_iota(jnp.int32, block.shape, 0) < 3
    pulls = split(jnp.where(place, x * mass, mass))
    pulls = jnp.concatenate([*pulls, jnp.zeros_like(x)], axis=0).astype(jnp.bfloat16)
    return features, pulls


def target_features(block, centre, grid):
    x = coordinates(block, centre)
    return rows_of(*pieces_of(x, grid, soften), False).astype(jnp.bfloat16)


def pair_pull(source, target, pulls):
    distance = jnp.dot(source, target, preferred_element_type=jnp.float32)
    inverse = lax.rsqrt(jnp.maximum(distance, soften))
    w = inverse * inverse * inverse
    high = w.astype(jnp.bfloat16)
    low = (w - high.astype(jnp.float32)).astype(jnp.bfloat16)
    return jnp.dot(
        jnp.concatenate([pulls, pulls], axis=1),
        jnp.concatenate([high, low], axis=0),
        preferred_element_type=jnp.float32,
    )


def running_count(chosen):
    rows, lanes = chosen.shape
    before = lax.broadcasted_iota(jnp.int32, (lanes, lanes), 0) <= lax.broadcasted_iota(jnp.int32, (lanes, lanes), 1)
    running = jnp.dot(
        jnp.where(chosen, 1.0, 0.0).astype(jnp.bfloat16),
        jnp.where(before, 1.0, 0.0).astype(jnp.bfloat16),
        preferred_element_type=jnp.float32,
    )
    ends = running[:, lanes - 1 : lanes]
    earlier = lax.broadcasted_iota(jnp.int32, (rows, rows), 1) < lax.broadcasted_iota(jnp.int32, (rows, rows), 0)
    offsets = jnp.dot(
        jnp.where(earlier, 1.0, 0.0).astype(jnp.bfloat16),
        jnp.broadcast_to(ends, (rows, lanes)).astype(jnp.bfloat16),
        preferred_element_type=jnp.float32,
    )
    return running + offsets, jnp.sum(ends, axis=0, keepdims=True)


def order_pairs(coded, radix, departures, own_blocks):
    rows, lanes = coded.shape
    total = rows * lanes
    place = lanes * lax.broadcasted_iota(jnp.int32, (rows, lanes), 0) + lax.broadcasted_iota(jnp.int32, (rows, lanes), 1)
    live = coded >= 0
    coded = jnp.maximum(coded, 0)
    pair_targets = coded // radix
    pair_sources = coded % radix
    own = live & (pair_sources < own_blocks)
    leaves = pair_targets == departures[0]
    for d in departures[1:]:
        leaves = leaves | (pair_targets == d)
    leaves = live & leaves & ~own
    own_count, own_total = running_count(own)
    leave_count, leave_total = running_count(leaves)
    slot = jnp.where(
        own,
        own_count - 1.0,
        jnp.where(
            leaves,
            own_total + leave_count - 1.0,
            own_total + leave_total + place.astype(jnp.float32) - own_count - leave_count,
        ),
    ).T
    digits = []
    for values in (pair_targets, pair_sources):
        digits += [(values // 128).astype(jnp.float32), (values % 128).astype(jnp.float32)]
    moved = jnp.zeros((8, total), jnp.float32)
    lane = lax.broadcasted_iota(jnp.int32, (lanes, total), 1).astype(jnp.float32)
    for r in range(rows):
        values = jnp.concatenate([d[r : r + 1] for d in digits] + [jnp.zeros((4, lanes), jnp.float32)], axis=0)
        here = jnp.where(slot[:, r : r + 1] == lane, 1.0, 0.0).astype(jnp.bfloat16)
        moved = moved + jnp.dot(values.astype(jnp.bfloat16), here, preferred_element_type=jnp.float32)
    targets = 128.0 * moved[0:1] + moved[1:2]
    sources = 128.0 * moved[2:3] + moved[3:4]
    live_total = jnp.sum(jnp.where(live, 1.0, 0.0), axis=1, keepdims=True)
    return targets, sources, own_total, leave_total, jnp.sum(live_total, axis=0, keepdims=True)


def early_groups(steps, limit):
    plan = []
    for k, (axis, stride) in enumerate(steps):
        groups = 0 if k == len(steps) - 1 else 1 if k == 0 or (axis, stride) == ("gz", 1) else 2
        plan.append(min(groups, limit - sum(plan)))
    return plan


def exchange_kernel(
    steps,
    plan,
    unroll,
    radix,
    coded_ref,
    select_vmem,
    moves_vmem,
    bodies_ref,
    pool_ref,
    sums_ref,
    order_ref,
    sources,
    pulls,
    targets,
    outgoing,
    arriving,
    parts,
    order,
    select_ref,
    moves_ref,
    send_sem,
    recv_sem,
    load_sem,
):
    own_blocks = bodies_ref.shape[0]
    send_count = outgoing.shape[1]
    partners = []
    for axis, stride in steps:
        me = lax.axis_index(axis)
        side = lax.rem(me // stride, 2)
        partners.append({axis: me + (1 - 2 * side) * stride})
    barrier = pltpu.get_barrier_semaphore()
    for partner in partners:
        pl.semaphore_signal(
            barrier, inc=1, device_id=partner, device_id_type=pl.DeviceIdType.MESH
        )
    load_select = pltpu.make_async_copy(select_vmem, select_ref, load_sem.at[0])
    load_moves = pltpu.make_async_copy(moves_vmem, moves_ref, load_sem.at[1])
    load_select.start()
    load_moves.start()
    pool_ref[0:own_blocks] = bodies_ref[...]
    centre, grid = frame_of(bodies_ref)
    batch = math.gcd(own_blocks, 12)

    @pl.loop(0, own_blocks // batch)
    def _(group):
        for b in [group * batch + u for u in range(batch)]:
            sources[b], pulls[b] = source_features(bodies_ref[b], centre, grid)
            targets[b] = target_features(bodies_ref[b], centre, grid)

    copies = [
        pltpu.make_async_remote_copy(
            src_ref=outgoing.at[k],
            dst_ref=arriving.at[k],
            send_sem=send_sem.at[k],
            recv_sem=recv_sem.at[k],
            device_id=partner,
            device_id_type=pl.DeviceIdType.MESH,
        )
        for k, partner in enumerate(partners)
    ]

    def send(k):
        for j in range(send_count):
            outgoing[k, j] = pool_ref[select_ref[k, 0, j]]
        copies[k].start()

    def receive(k):
        copies[k].wait_recv()
        base = own_blocks + k * send_count
        pool_ref[base : base + send_count] = arriving[k]

    def prepare(k):
        half = math.gcd(send_count, 8)

        @pl.loop(0, send_count // half)
        def _(group):
            for b in [own_blocks + k * send_count + group * half + u for u in range(half)]:
                sources[b], pulls[b] = source_features(pool_ref[b], centre, grid)

    load_select.wait()
    load_moves.wait()
    pl.semaphore_wait(barrier, len(partners))
    send(0)
    departures = [moves_ref[0, m] // moves_radix for m in range(moves_ref.shape[1])]
    row_t, row_s, *totals = order_pairs(coded_ref[...], radix, departures, own_blocks)
    own_total = totals[0]
    slots = row_t.shape[1]
    table = [row_t, row_s, *[jnp.broadcast_to(total, row_t.shape) for total in totals]]
    table = jnp.concatenate([*table, jnp.zeros((8 - len(table), slots), jnp.float32)], axis=0)
    order_ref[...] = table.astype(jnp.int32)
    into_order = pltpu.make_async_copy(order_ref, order, load_sem.at[0])
    into_order.start()
    into_order.wait()

    @pl.loop(0, sum(plan))
    def _(group):
        for k in range(1, len(partners)):

            @pl.when(group == sum(plan[:k]))
            def _():
                receive(k - 1)
                send(k)
                prepare(k - 1)

        for u in range(unroll):
            p = group * unroll + u
            t = jnp.clip(order[0, p], 0, own_blocks - 1)
            s = jnp.clip(order[1, p], 0, own_blocks - 1)
            pull = pair_pull(sources[s], targets[t], pulls[s])
            parts[p] = pull[0:8] + pull[8:16]

    for k in range(1, len(partners)):
        if sum(plan[:k]) >= sum(plan):
            receive(k - 1)
            send(k)
            prepare(k - 1)
    early = parts.shape[0]
    members = lax.broadcasted_iota(jnp.int32, (-(-own_blocks // 16) * 16, early), 0)
    spot = lax.broadcasted_iota(jnp.int32, members.shape, 1).astype(jnp.float32)
    chosen = (members == order_ref[0:1, 0:early]) & (spot < own_total)
    chosen = jnp.where(chosen, 1.0, 0.0).astype(jnp.bfloat16)
    for c in range(4):
        total = jnp.zeros((members.shape[0], parts.shape[2]), jnp.float32)
        for piece in split(parts[:, c, :] + parts[:, c + 4, :]):
            total = total + jnp.dot(chosen, piece.astype(jnp.bfloat16), preferred_element_type=jnp.float32)
        sums_ref[:, c, :] = total[0:own_blocks]
    receive(len(partners) - 1)
    prepare(len(partners) - 1)
    for copy in copies:
        copy.wait_send()


def pull_loop(first, last, order_ref, sources, targets, pulls, sums, unroll):
    slots = order_ref.shape[1]
    nowhere = sums.shape[0] - 1

    @pl.loop(0, (last - first + unroll - 1) // unroll)
    def _(group):
        for u in range(unroll):
            p = first + group * unroll + u
            live = p < last
            p = jnp.minimum(p, slots - 1)
            t = order_ref[0, p]
            s = order_ref[1, p]
            where = jnp.where(live, t, nowhere)
            sums[where] += pair_pull(sources[s], targets[t], pulls[s])


def update(b, centre, pool_ref, sums, velocity_ref):
    total = sums[b, 0:4] + sums[b, 4:8] + sums[b, 8:12]
    block = pool_ref[b]
    pull = total - coordinates(block, centre) * total[3:4]
    places, velocities = [], []
    for c in range(3):
        velocity_new = velocity_ref[c, pl.ds(b, 1), :] + timestep * pull[c : c + 1]
        velocities.append(velocity_new)
        places.append(block[c : c + 1, :] + timestep * velocity_new)
    return [*places, block[3:4, :], *velocities]


def leaving_range(order_ref, early, unroll):
    first = jnp.minimum(order_ref[2, 0], early)
    groups = (order_ref[2, 0] + order_ref[3, 0] - first + unroll - 1) // unroll
    return first, jnp.minimum(first + groups * unroll, order_ref[4, 0])


def leaving_kernel(
    unroll,
    early,
    order_ref,
    moves_ref,
    pool_ref,
    early_sums_ref,
    velocity_ref,
    sources,
    pulls,
    targets,
    sums,
    *rest,
):
    outboxes, (boxes, used) = rest[:-2], rest[-2:]
    own_blocks = early_sums_ref.shape[0]
    span = pool_ref.shape[2]
    centre, _ = frame_of(pool_ref.at[pl.ds(0, own_blocks)])
    sums[0:own_blocks, 0:4] = early_sums_ref[...]
    sums[0:own_blocks, 4:16] = jnp.zeros((own_blocks, 12, span), jnp.float32)
    sums[own_blocks] = jnp.zeros(sums.shape[1:], jnp.float32)
    boxes[...] = jnp.zeros_like(boxes)
    for g in range(used.shape[0]):
        used[g] = 0
    pull_loop(*leaving_range(order_ref, early, unroll), order_ref, sources, targets, pulls, sums, unroll)
    me = lax.axis_index("gz")
    for m in range(moves_ref.shape[1]):
        owner = moves_ref[0, m] % moves_radix
        slot = used[owner]
        used[owner] = slot + 1
        box = jnp.bitwise_xor(owner, me)
        for c, row in enumerate(update(moves_ref[0, m] // moves_radix, centre, pool_ref, sums, velocity_ref)):
            boxes[box, slot, c : c + 1, :] = row
    for g, outbox in enumerate(outboxes):
        outbox[...] = boxes[g]


def staying_kernel(
    unroll,
    early,
    order_ref,
    moves_ref,
    pool_ref,
    sums_ref,
    velocity_ref,
    sources,
    pulls,
    targets,
    resident_ref,
    sums,
):
    own_blocks = sums_ref.shape[0] - 1
    span = pool_ref.shape[2]
    centre, _ = frame_of(pool_ref.at[pl.ds(0, own_blocks)])
    sums[...] = sums_ref[...]
    _, first = leaving_range(order_ref, early, unroll)
    pull_loop(first, order_ref[4, 0], order_ref, sources, targets, pulls, sums, unroll)
    batch = math.gcd(own_blocks, 12)

    @pl.loop(0, own_blocks // batch)
    def _(group):
        for b in [group * batch + u for u in range(batch)]:
            for c, row in enumerate(update(b, centre, pool_ref, sums, velocity_ref)):
                resident_ref[c, pl.ds(b, 1), :] = row

    for m in range(moves_ref.shape[1]):
        for c in range(resident_ref.shape[0]):
            resident_ref[c, pl.ds(moves_ref[0, m] // moves_radix, 1), :] = jnp.zeros((1, span), jnp.float32)


def inbox_kernel(*refs):
    boxes, moved_ref = refs[:-1], refs[-1]
    me = lax.axis_index("gz")
    slot_total = boxes[0].shape[0]
    for g, box in enumerate(boxes):
        sender = jnp.bitwise_xor(me, g)
        for slot in range(slot_total):
            for c in range(moved_ref.shape[0]):
                moved_ref[c, pl.ds(sender * slot_total + slot, 1), :] = box[slot, c : c + 1, :]


def on_device(bodies, velocity, select, pair_target, pair_source, counts, departures, owners):
    own_blocks = bodies.shape[0]
    span = bodies.shape[2]
    smem = pl.BlockSpec(memory_space=pltpu.SMEM)
    vmem = pl.BlockSpec(memory_space=pltpu.VMEM)
    steps = [
        (axis, 2**bit)
        for axis in ("gx", "gy", "gz")
        for bit in range(lax.axis_size(axis).bit_length() - 1)
    ]
    send_count = select.shape[2]
    slab = pltpu.VMEM((len(steps), send_count, 4, span), jnp.float32)
    slots = pair_target.shape[1]
    unroll = math.gcd(slots, deepest_unroll)
    plan = early_groups(steps, slots // unroll)
    early = sum(plan) * unroll
    pool_size = own_blocks + len(steps) * send_count
    move_count = departures.shape[1]
    radix = 1 << (pool_size - 1).bit_length()
    place = lax.broadcasted_iota(jnp.int32, pair_target.shape, 1)
    coded = jnp.where(place < counts[None, :], pair_target * radix + pair_source, -1).reshape(slots // 128, 128)
    moves = departures * moves_radix + jnp.transpose(owners, (1, 0))
    velocity = jnp.transpose(velocity, (1, 0, 2))
    pool, early_sums, order, sources, pulls, targets = pl.pallas_call(
        functools.partial(exchange_kernel, steps, plan, unroll, radix),
        out_shape=(
            jax.ShapeDtypeStruct((pool_size, 4, span), jnp.float32),
            jax.ShapeDtypeStruct((own_blocks, 4, span), jnp.float32),
            jax.ShapeDtypeStruct((8, slots), jnp.int32),
            jax.ShapeDtypeStruct((pool_size, span, 64), jnp.bfloat16),
            jax.ShapeDtypeStruct((pool_size, 16, span), jnp.bfloat16),
            jax.ShapeDtypeStruct((own_blocks, 64, span), jnp.bfloat16),
        ),
        in_specs=[vmem] * 4,
        out_specs=(vmem,) * 6,
        scratch_shapes=[
            slab,
            slab,
            pltpu.VMEM((early, 8, span), jnp.float32),
            pltpu.SMEM((8, slots), jnp.int32),
            pltpu.SMEM((len(steps), 1, send_count), jnp.int32),
            pltpu.SMEM((1, move_count), jnp.int32),
            pltpu.SemaphoreType.DMA((len(steps),)),
            pltpu.SemaphoreType.DMA((len(steps),)),
            pltpu.SemaphoreType.DMA((2,)),
        ],
        compiler_params=pltpu.CompilerParams(
            collective_id=0, has_side_effects=True, vmem_limit_bytes=32 << 20
        ),
        cost_estimate=pl.CostEstimate(flops=10**10, bytes_accessed=1048576, transcendentals=0),
        name="exchange",
    )(coded, jnp.transpose(select, (1, 0, 2)), moves, bodies)
    group_size = lax.axis_size("gz")
    slot_total = max(2, 2 * move_count // group_size)
    work = pl.CostEstimate(flops=20 * slots // 4 * span * span, bytes_accessed=1 << 20, transcendentals=0)
    box = jax.ShapeDtypeStruct((slot_total, 7, span), jnp.float32)
    sums, *outboxes = pl.pallas_call(
        functools.partial(leaving_kernel, unroll, early),
        out_shape=(jax.ShapeDtypeStruct((own_blocks + 1, 16, span), jnp.float32),) + (box,) * group_size,
        in_specs=[smem, smem] + [vmem] * 6,
        out_specs=(vmem,) * (1 + group_size),
        scratch_shapes=[
            pltpu.VMEM((group_size, slot_total, 7, span), jnp.float32),
            pltpu.SMEM((group_size,), jnp.int32),
        ],
        compiler_params=pltpu.CompilerParams(vmem_limit_bytes=24 << 20),
        name="leaving",
    )(order, moves, pool, early_sums, velocity, sources, pulls, targets)
    inboxes = [outboxes[0]]
    for g in range(1, group_size):
        pairs = [(i, i ^ g) for i in range(group_size)]
        inboxes.append(lax.ppermute(outboxes[g], "gz", pairs))
    resident = pl.pallas_call(
        functools.partial(staying_kernel, unroll, early),
        out_shape=jax.ShapeDtypeStruct((7, own_blocks, span), jnp.float32),
        in_specs=[smem, smem] + [vmem] * 6,
        out_specs=vmem,
        scratch_shapes=[pltpu.VMEM((own_blocks + 1, 16, span), jnp.float32)],
        compiler_params=pltpu.CompilerParams(vmem_limit_bytes=24 << 20),
        cost_estimate=work,
        name="staying",
    )(order, moves, pool, sums, velocity, sources, pulls, targets)
    moved = pl.pallas_call(
        inbox_kernel,
        out_shape=jax.ShapeDtypeStruct((7, group_size * slot_total, span), jnp.float32),
        in_specs=[vmem] * group_size,
        out_specs=vmem,
        compiler_params=pltpu.CompilerParams(vmem_limit_bytes=16 << 20),
        name="inbox",
    )(*inboxes)
    return jnp.transpose(resident, (1, 0, 2)), jnp.transpose(moved, (1, 0, 2))


def solution(mesh):
    everywhere = ("gx", "gy", "gz")
    cube = P(everywhere, None, None)
    flat = P(everywhere, None)
    return jax.shard_map(
        on_device,
        mesh=mesh,
        in_specs=(cube, cube, cube, flat, flat, P(everywhere), flat, flat),
        out_specs=(cube, cube),
        check_vma=False,
    )
```

```python
import functools
import math

import jax
import jax.numpy as jnp
from jax import lax
from jax.experimental import pallas as pl
from jax.experimental.pallas import tpu as pltpu
from jax.sharding import PartitionSpec as P

soften = 0.01
timestep = 0.25
deepest_unroll = 64
moves_radix = 1 << 16
coarse = 2.0**14.5


def split(values):
    high = values.astype(jnp.bfloat16).astype(jnp.float32)
    rest = values - high
    middle = rest.astype(jnp.bfloat16).astype(jnp.float32)
    return high, middle, rest - middle


def frame_of(own_ref):
    lowest = jnp.min(own_ref[...], axis=0)
    highest = jnp.max(own_ref[...], axis=0)
    lowest = jnp.min(lowest, axis=1, keepdims=True)
    highest = jnp.max(highest, axis=1, keepdims=True)
    place = lax.broadcasted_iota(jnp.int32, lowest.shape, 0) < 3
    centre = jnp.where(place, 0.5 * lowest + 0.5 * highest, 0.0)
    reach = jnp.where(place, 0.5 * highest - 0.5 * lowest, 0.0)
    reach = jnp.max(reach, axis=0, keepdims=True)
    return centre, reach * coarse


def coordinates(block, centre):
    place = lax.broadcasted_iota(jnp.int32, block.shape, 0) < 3
    return jnp.where(place, block - centre, 0.0)


def pieces_of(x, grid, extra):
    coarse_x = (x + grid) - grid
    fine_x = x - coarse_x
    g1 = coarse_x.astype(jnp.bfloat16).astype(jnp.float32)
    g2 = coarse_x - g1
    f1 = fine_x.astype(jnp.bfloat16).astype(jnp.float32)
    f2 = fine_x - f1
    norm = jnp.sum(coarse_x * coarse_x, axis=0, keepdims=True)
    rest = jnp.sum(fine_x * (2.0 * coarse_x + fine_x), axis=0, keepdims=True) + extra
    return (g1, g2, f1, f2), (*split(norm), *split(rest))


meetings = ((0, 0), (0, 1), (1, 0), (1, 1), (0, 2), (2, 0), (1, 2), (2, 1), (0, 3), (3, 0), (1, 3), (3, 1), (2, 2), (2, 3), (3, 2))


def rows_of(pieces, norms, source):
    place = lax.broadcasted_iota(jnp.int32, pieces[0].shape, 0) < 3
    one = jnp.ones_like(norms[0])
    rows = []
    for n, (from_source, from_target) in enumerate(meetings):
        if n >= 2 * len(norms):
            fill = jnp.zeros_like(one)
        elif (n % 2 == 0) == source:
            fill = norms[n // 2]
        else:
            fill = one
        mine = pieces[from_source] if source else -2.0 * pieces[from_target]
        rows.append(jnp.where(place, mine, fill))
    rows.append(jnp.zeros_like(rows[0]))
    return jnp.concatenate(rows, axis=0)


def source_features(block, centre, grid):
    x = coordinates(block, centre)
    features = rows_of(*pieces_of(x, grid, 0.0), True).T.astype(jnp.bfloat16)
    mass = block[3:4]
    place = lax.broadcasted_iota(jnp.int32, block.shape, 0) < 3
    pulls = split(jnp.where(place, x * mass, mass))
    pulls = jnp.concatenate([*pulls, jnp.zeros_like(x)], axis=0).astype(jnp.bfloat16)
    return features, pulls


def target_features(block, centre, grid):
    x = coordinates(block, centre)
    return rows_of(*pieces_of(x, grid, soften), False).astype(jnp.bfloat16)


def pair_pull(source, target, pulls):
    distance = jnp.dot(source, target, preferred_element_type=jnp.float32)
    inverse = lax.rsqrt(jnp.maximum(distance, soften))
    w = inverse * inverse * inverse
    high = w.astype(jnp.bfloat16)
    low = (w - high.astype(jnp.float32)).astype(jnp.bfloat16)
    return jnp.dot(
        jnp.concatenate([pulls, pulls], axis=1),
        jnp.concatenate([high, low], axis=0),
        preferred_element_type=jnp.float32,
    )


def running_count(chosen):
    rows, lanes = chosen.shape
    before = lax.broadcasted_iota(jnp.int32, (lanes, lanes), 0) <= lax.broadcasted_iota(jnp.int32, (lanes, lanes), 1)
    running = jnp.dot(
        jnp.where(chosen, 1.0, 0.0).astype(jnp.bfloat16),
        jnp.where(before, 1.0, 0.0).astype(jnp.bfloat16),
        preferred_element_type=jnp.float32,
    )
    ends = running[:, lanes - 1 : lanes]
    earlier = lax.broadcasted_iota(jnp.int32, (rows, rows), 1) < lax.broadcasted_iota(jnp.int32, (rows, rows), 0)
    offsets = jnp.dot(
        jnp.where(earlier, 1.0, 0.0).astype(jnp.bfloat16),
        jnp.broadcast_to(ends, (rows, lanes)).astype(jnp.bfloat16),
        preferred_element_type=jnp.float32,
    )
    return running + offsets, jnp.sum(ends, axis=0, keepdims=True)


def order_pairs(coded, radix, departures, own_blocks):
    rows, lanes = coded.shape
    total = rows * lanes
    place = lanes * lax.broadcasted_iota(jnp.int32, (rows, lanes), 0) + lax.broadcasted_iota(jnp.int32, (rows, lanes), 1)
    live = coded >= 0
    coded = jnp.maximum(coded, 0)
    pair_targets = coded // radix
    pair_sources = coded % radix
    own = live & (pair_sources < own_blocks)
    leaves = pair_targets == departures[0]
    for d in departures[1:]:
        leaves = leaves | (pair_targets == d)
    leaves = live & leaves & ~own
    own_count, own_total = running_count(own)
    leave_count, leave_total = running_count(leaves)
    slot = jnp.where(
        own,
        own_count - 1.0,
        jnp.where(
            leaves,
            own_total + leave_count - 1.0,
            own_total + leave_total + place.astype(jnp.float32) - own_count - leave_count,
        ),
    ).T
    digits = []
    for values in (pair_targets, pair_sources):
        digits += [(values // 128).astype(jnp.float32), (values % 128).astype(jnp.float32)]
    moved = jnp.zeros((8, total), jnp.float32)
    lane = lax.broadcasted_iota(jnp.int32, (lanes, total), 1).astype(jnp.float32)
    for r in range(rows):
        values = jnp.concatenate([d[r : r + 1] for d in digits] + [jnp.zeros((4, lanes), jnp.float32)], axis=0)
        here = jnp.where(slot[:, r : r + 1] == lane, 1.0, 0.0).astype(jnp.bfloat16)
        moved = moved + jnp.dot(values.astype(jnp.bfloat16), here, preferred_element_type=jnp.float32)
    targets = 128.0 * moved[0:1] + moved[1:2]
    sources = 128.0 * moved[2:3] + moved[3:4]
    live_total = jnp.sum(jnp.where(live, 1.0, 0.0), axis=1, keepdims=True)
    return targets, sources, own_total, leave_total, jnp.sum(live_total, axis=0, keepdims=True)


def early_groups(steps, limit):
    plan = []
    for k, (axis, stride) in enumerate(steps):
        groups = 0 if k == 1 else 1 if (axis, stride) == ("gz", 1) else 2
        plan.append(min(groups, limit - sum(plan)))
    return plan


def exchange_kernel(
    steps,
    plan,
    unroll,
    radix,
    coded_ref,
    select_vmem,
    moves_vmem,
    bodies_ref,
    pool_ref,
    sums_ref,
    order_ref,
    sources,
    pulls,
    targets,
    outgoing,
    arriving,
    passed,
    chosen_vmem,
    chosen_ref,
    parts,
    order,
    select_ref,
    moves_ref,
    send_sem,
    recv_sem,
    load_sem,
):
    own_blocks = bodies_ref.shape[0]
    send_count = outgoing.shape[1]
    partners = []
    for axis, stride in steps:
        me = lax.axis_index(axis)
        side = lax.rem(me // stride, 2)
        partners.append({axis: me + (1 - 2 * side) * stride})
    across = dict(partners[0])
    for axis, place in partners[1].items():
        across[axis] = across[axis] + place - lax.axis_index(axis) if axis in across else place
    barrier = pltpu.get_barrier_semaphore()
    for partner in [*partners, across]:
        pl.semaphore_signal(
            barrier, inc=1, device_id=partner, device_id_type=pl.DeviceIdType.MESH
        )
    load_select = pltpu.make_async_copy(select_vmem, select_ref, load_sem.at[0])
    load_moves = pltpu.make_async_copy(moves_vmem, moves_ref, load_sem.at[1])
    load_select.start()
    load_moves.start()
    pool_ref[0:own_blocks] = bodies_ref[...]
    centre, grid = frame_of(bodies_ref)
    batch = math.gcd(own_blocks, 12)

    @pl.loop(0, own_blocks // batch)
    def _(group):
        for b in [group * batch + u for u in range(batch)]:
            sources[b], pulls[b] = source_features(bodies_ref[b], centre, grid)
            targets[b] = target_features(bodies_ref[b], centre, grid)

    def remote(source, target, n, partner):
        return pltpu.make_async_remote_copy(
            src_ref=source,
            dst_ref=target,
            send_sem=send_sem.at[n],
            recv_sem=recv_sem.at[n],
            device_id=partner,
            device_id_type=pl.DeviceIdType.MESH,
        )

    hops = len(partners)
    copies = [remote(outgoing.at[k], arriving.at[k], k, partner) for k, partner in enumerate(partners)]
    copies.append(remote(outgoing.at[0], passed, hops, across))
    copies.append(remote(select_vmem.at[1], chosen_vmem, hops + 1, partners[1]))

    def send_first():
        for j in range(send_count):
            outgoing[0, j] = pool_ref[select_ref[0, 0, j]]
            outgoing[1, j] = pool_ref[jnp.minimum(select_ref[1, 0, j], own_blocks - 1)]
        for copy in (copies[0], copies[hops], copies[1], copies[hops + 1]):
            copy.start()

    def send(k):
        for j in range(send_count):
            outgoing[k, j] = pool_ref[select_ref[k, 0, j]]
        copies[k].start()

    def receive(k):
        base = own_blocks + k * send_count
        if k == 1:
            copies[hops + 1].wait_recv()
            load_chosen = pltpu.make_async_copy(chosen_vmem, chosen_ref, load_sem.at[2])
            load_chosen.start()
            for copy in (copies[0], copies[hops], copies[1]):
                copy.wait_recv()
            pool_ref[own_blocks:base] = arriving[0]
            load_chosen.wait()
            for j in range(send_count):
                place = chosen_ref[0, j]
                theirs = passed[jnp.clip(place - own_blocks, 0, send_count - 1)]
                pool_ref[base + j] = jnp.where(place < own_blocks, arriving[1, j], theirs)
        else:
            copies[k].wait_recv()
            pool_ref[base : base + send_count] = arriving[k]

    def prepare(k):
        half = math.gcd(send_count, 8)

        @pl.loop(0, send_count // half)
        def _(group):
            for b in [own_blocks + k * send_count + group * half + u for u in range(half)]:
                sources[b], pulls[b] = source_features(pool_ref[b], centre, grid)

    load_select.wait()
    load_moves.wait()
    pl.semaphore_wait(barrier, len(partners) + 1)
    send_first()
    departures = [moves_ref[0, m] // moves_radix for m in range(moves_ref.shape[1])]
    row_t, row_s, *totals = order_pairs(coded_ref[...], radix, departures, own_blocks)
    own_total = totals[0]
    slots = row_t.shape[1]
    table = [row_t, row_s, *[jnp.broadcast_to(total, row_t.shape) for total in totals]]
    table = jnp.concatenate([*table, jnp.zeros((8 - len(table), slots), jnp.float32)], axis=0)
    order_ref[...] = table.astype(jnp.int32)
    into_order = pltpu.make_async_copy(order_ref, order, load_sem.at[0])
    into_order.start()
    into_order.wait()

    @pl.loop(0, sum(plan))
    def _(group):
        for k in range(2, len(partners)):

            @pl.when(group == sum(plan[:k]))
            def _():
                receive(k - 1)
                send(k)
                if k == 2:
                    prepare(0)
                prepare(k - 1)

        for u in range(unroll):
            p = group * unroll + u
            t = jnp.clip(order[0, p], 0, own_blocks - 1)
            s = jnp.clip(order[1, p], 0, own_blocks - 1)
            pull = pair_pull(sources[s], targets[t], pulls[s])
            pull = pull[0:4] + pull[4:8] + pull[8:12]
            for c in range(4):
                parts[c, pl.ds(p, 1), :] = pull[c : c + 1]

    for k in range(2, len(partners)):
        if sum(plan[:k]) >= sum(plan):
            receive(k - 1)
            send(k)
            if k == 2:
                prepare(0)
            prepare(k - 1)
    early = parts.shape[1]
    members = lax.broadcasted_iota(jnp.int32, (-(-own_blocks // 16) * 16, early), 0)
    spot = lax.broadcasted_iota(jnp.int32, members.shape, 1).astype(jnp.float32)
    chosen = (members == order_ref[0:1, 0:early]) & (spot < own_total)
    chosen = jnp.where(chosen, 1.0, 0.0).astype(jnp.bfloat16)
    for c in range(4):
        total = jnp.zeros((members.shape[0], parts.shape[2]), jnp.float32)
        for piece in split(parts[c]):
            total = total + jnp.dot(chosen, piece.astype(jnp.bfloat16), preferred_element_type=jnp.float32)
        sums_ref[:, c, :] = total[0:own_blocks]
    receive(len(partners) - 1)
    prepare(len(partners) - 1)
    for copy in copies:
        copy.wait_send()


def pull_loop(first, last, order_ref, sources, targets, pulls, sums, unroll):
    slots = order_ref.shape[1]
    nowhere = sums.shape[0] - 1

    @pl.loop(0, (last - first + unroll - 1) // unroll)
    def _(group):
        for u in range(unroll):
            p = first + group * unroll + u
            live = p < last
            p = jnp.minimum(p, slots - 1)
            t = order_ref[0, p]
            s = order_ref[1, p]
            where = jnp.where(live, t, nowhere)
            sums[where] += pair_pull(sources[s], targets[t], pulls[s])


def update(b, centre, pool_ref, sums, velocity_ref):
    total = sums[b, 0:4] + sums[b, 4:8] + sums[b, 8:12]
    block = pool_ref[b]
    pull = total - coordinates(block, centre) * total[3:4]
    places, velocities = [], []
    for c in range(3):
        velocity_new = velocity_ref[c, pl.ds(b, 1), :] + timestep * pull[c : c + 1]
        velocities.append(velocity_new)
        places.append(block[c : c + 1, :] + timestep * velocity_new)
    return [*places, block[3:4, :], *velocities]


def leaving_range(order_ref, early, unroll):
    first = jnp.minimum(order_ref[2, 0], early)
    groups = (order_ref[2, 0] + order_ref[3, 0] - first + unroll - 1) // unroll
    return first, jnp.minimum(first + groups * unroll, order_ref[4, 0])


def leaving_kernel(
    unroll,
    early,
    order_ref,
    moves_ref,
    pool_ref,
    early_sums_ref,
    velocity_ref,
    sources,
    pulls,
    targets,
    sums,
    *rest,
):
    outboxes, (boxes, used) = rest[:-2], rest[-2:]
    own_blocks = early_sums_ref.shape[0]
    span = pool_ref.shape[2]
    centre, _ = frame_of(pool_ref.at[pl.ds(0, own_blocks)])
    sums[0:own_blocks, 0:4] = early_sums_ref[...]
    sums[0:own_blocks, 4:16] = jnp.zeros((own_blocks, 12, span), jnp.float32)
    sums[own_blocks] = jnp.zeros(sums.shape[1:], jnp.float32)
    boxes[...] = jnp.zeros_like(boxes)
    for g in range(used.shape[0]):
        used[g] = 0
    pull_loop(*leaving_range(order_ref, early, unroll), order_ref, sources, targets, pulls, sums, unroll)
    me = lax.axis_index("gz")
    for m in range(moves_ref.shape[1]):
        owner = moves_ref[0, m] % moves_radix
        slot = used[owner]
        used[owner] = slot + 1
        box = jnp.bitwise_xor(owner, me)
        for c, row in enumerate(update(moves_ref[0, m] // moves_radix, centre, pool_ref, sums, velocity_ref)):
            boxes[box, slot, c : c + 1, :] = row
    for g, outbox in enumerate(outboxes):
        outbox[...] = boxes[g]


def staying_kernel(
    unroll,
    early,
    order_ref,
    moves_ref,
    pool_ref,
    sums_ref,
    velocity_ref,
    sources,
    pulls,
    targets,
    resident_ref,
    sums,
):
    own_blocks = sums_ref.shape[0] - 1
    span = pool_ref.shape[2]
    centre, _ = frame_of(pool_ref.at[pl.ds(0, own_blocks)])
    sums[...] = sums_ref[...]
    _, first = leaving_range(order_ref, early, unroll)
    pull_loop(first, order_ref[4, 0], order_ref, sources, targets, pulls, sums, unroll)
    batch = math.gcd(own_blocks, 12)

    @pl.loop(0, own_blocks // batch)
    def _(group):
        for b in [group * batch + u for u in range(batch)]:
            for c, row in enumerate(update(b, centre, pool_ref, sums, velocity_ref)):
                resident_ref[c, pl.ds(b, 1), :] = row

    for m in range(moves_ref.shape[1]):
        for c in range(resident_ref.shape[0]):
            resident_ref[c, pl.ds(moves_ref[0, m] // moves_radix, 1), :] = jnp.zeros((1, span), jnp.float32)


def inbox_kernel(*refs):
    boxes, moved_ref = refs[:-1], refs[-1]
    me = lax.axis_index("gz")
    slot_total = boxes[0].shape[0]
    for g, box in enumerate(boxes):
        sender = jnp.bitwise_xor(me, g)
        for slot in range(slot_total):
            for c in range(moved_ref.shape[0]):
                moved_ref[c, pl.ds(sender * slot_total + slot, 1), :] = box[slot, c : c + 1, :]


def on_device(bodies, velocity, select, pair_target, pair_source, counts, departures, owners):
    own_blocks = bodies.shape[0]
    span = bodies.shape[2]
    smem = pl.BlockSpec(memory_space=pltpu.SMEM)
    vmem = pl.BlockSpec(memory_space=pltpu.VMEM)
    steps = [
        (axis, 2**bit)
        for axis in ("gx", "gy", "gz")
        for bit in range(lax.axis_size(axis).bit_length() - 1)
    ]
    send_count = select.shape[2]
    slab = pltpu.VMEM((len(steps), send_count, 4, span), jnp.float32)
    slots = pair_target.shape[1]
    unroll = math.gcd(slots, deepest_unroll)
    plan = early_groups(steps, slots // unroll)
    early = sum(plan) * unroll
    pool_size = own_blocks + len(steps) * send_count
    move_count = departures.shape[1]
    radix = 1 << (pool_size - 1).bit_length()
    place = lax.broadcasted_iota(jnp.int32, pair_target.shape, 1)
    coded = jnp.where(place < counts[None, :], pair_target * radix + pair_source, -1).reshape(slots // 128, 128)
    moves = departures * moves_radix + jnp.transpose(owners, (1, 0))
    velocity = jnp.transpose(velocity, (1, 0, 2))
    pool, early_sums, order, sources, pulls, targets = pl.pallas_call(
        functools.partial(exchange_kernel, steps, plan, unroll, radix),
        out_shape=(
            jax.ShapeDtypeStruct((pool_size, 4, span), jnp.float32),
            jax.ShapeDtypeStruct((own_blocks, 4, span), jnp.float32),
            jax.ShapeDtypeStruct((8, slots), jnp.int32),
            jax.ShapeDtypeStruct((pool_size, span, 64), jnp.bfloat16),
            jax.ShapeDtypeStruct((pool_size, 16, span), jnp.bfloat16),
            jax.ShapeDtypeStruct((own_blocks, 64, span), jnp.bfloat16),
        ),
        in_specs=[vmem] * 4,
        out_specs=(vmem,) * 6,
        scratch_shapes=[
            slab,
            slab,
            pltpu.VMEM((send_count, 4, span), jnp.float32),
            pltpu.VMEM((1, send_count), jnp.int32),
            pltpu.SMEM((1, send_count), jnp.int32),
            pltpu.VMEM((4, early, span), jnp.float32),
            pltpu.SMEM((8, slots), jnp.int32),
            pltpu.SMEM((len(steps), 1, send_count), jnp.int32),
            pltpu.SMEM((1, move_count), jnp.int32),
            pltpu.SemaphoreType.DMA((len(steps) + 2,)),
            pltpu.SemaphoreType.DMA((len(steps) + 2,)),
            pltpu.SemaphoreType.DMA((3,)),
        ],
        compiler_params=pltpu.CompilerParams(
            collective_id=0, has_side_effects=True, vmem_limit_bytes=32 << 20
        ),
        cost_estimate=pl.CostEstimate(flops=10**10, bytes_accessed=1048576, transcendentals=0),
        name="exchange",
    )(coded, jnp.transpose(select, (1, 0, 2)), moves, bodies)
    group_size = lax.axis_size("gz")
    slot_total = max(2, 2 * move_count // group_size)
    work = pl.CostEstimate(flops=20 * slots // 4 * span * span, bytes_accessed=1 << 20, transcendentals=0)
    box = jax.ShapeDtypeStruct((slot_total, 7, span), jnp.float32)
    sums, *outboxes = pl.pallas_call(
        functools.partial(leaving_kernel, unroll, early),
        out_shape=(jax.ShapeDtypeStruct((own_blocks + 1, 16, span), jnp.float32),) + (box,) * group_size,
        in_specs=[smem, smem] + [vmem] * 6,
        out_specs=(vmem,) * (1 + group_size),
        scratch_shapes=[
            pltpu.VMEM((group_size, slot_total, 7, span), jnp.float32),
            pltpu.SMEM((group_size,), jnp.int32),
        ],
        compiler_params=pltpu.CompilerParams(vmem_limit_bytes=24 << 20),
        name="leaving",
    )(order, moves, pool, early_sums, velocity, sources, pulls, targets)
    inboxes = [outboxes[0]]
    for g in range(1, group_size):
        pairs = [(i, i ^ g) for i in range(group_size)]
        inboxes.append(lax.ppermute(outboxes[g], "gz", pairs))
    resident = pl.pallas_call(
        functools.partial(staying_kernel, unroll, early),
        out_shape=jax.ShapeDtypeStruct((7, own_blocks, span), jnp.float32),
        in_specs=[smem, smem] + [vmem] * 6,
        out_specs=vmem,
        scratch_shapes=[pltpu.VMEM((own_blocks + 1, 16, span), jnp.float32)],
        compiler_params=pltpu.CompilerParams(vmem_limit_bytes=24 << 20),
        cost_estimate=work,
        name="staying",
    )(order, moves, pool, sums, velocity, sources, pulls, targets)
    moved = pl.pallas_call(
        inbox_kernel,
        out_shape=jax.ShapeDtypeStruct((7, group_size * slot_total, span), jnp.float32),
        in_specs=[vmem] * group_size,
        out_specs=vmem,
        compiler_params=pltpu.CompilerParams(vmem_limit_bytes=16 << 20),
        name="inbox",
    )(*inboxes)
    return jnp.transpose(resident, (1, 0, 2)), jnp.transpose(moved, (1, 0, 2))


def solution(mesh):
    everywhere = ("gx", "gy", "gz")
    cube = P(everywhere, None, None)
    flat = P(everywhere, None)
    return jax.shard_map(
        on_device,
        mesh=mesh,
        in_specs=(cube, cube, cube, flat, flat, P(everywhere), flat, flat),
        out_specs=(cube, cube),
        check_vma=False,
    )
```

```python
import functools
import math

import jax
import jax.numpy as jnp
from jax import lax
from jax.experimental import pallas as pl
from jax.experimental.pallas import tpu as pltpu
from jax.sharding import PartitionSpec as P

soften = 0.01
timestep = 0.25
deepest_unroll = 64
moves_radix = 1 << 16
coarse = 2.0**14.5


def split(values):
    high = values.astype(jnp.bfloat16).astype(jnp.float32)
    rest = values - high
    middle = rest.astype(jnp.bfloat16).astype(jnp.float32)
    return high, middle, rest - middle


def frame_of(own_ref):
    lowest = jnp.min(own_ref[...], axis=0)
    highest = jnp.max(own_ref[...], axis=0)
    lowest = jnp.min(lowest, axis=1, keepdims=True)
    highest = jnp.max(highest, axis=1, keepdims=True)
    place = lax.broadcasted_iota(jnp.int32, lowest.shape, 0) < 3
    centre = jnp.where(place, 0.5 * lowest + 0.5 * highest, 0.0)
    reach = jnp.where(place, 0.5 * highest - 0.5 * lowest, 0.0)
    reach = jnp.max(reach, axis=0, keepdims=True)
    return centre, reach * coarse


def coordinates(block, centre):
    place = lax.broadcasted_iota(jnp.int32, block.shape, 0) < 3
    return jnp.where(place, block - centre, 0.0)


def pieces_of(x, grid, extra):
    coarse_x = (x + grid) - grid
    fine_x = x - coarse_x
    g1 = coarse_x.astype(jnp.bfloat16).astype(jnp.float32)
    g2 = coarse_x - g1
    f1 = fine_x.astype(jnp.bfloat16).astype(jnp.float32)
    f2 = fine_x - f1
    norm = jnp.sum(coarse_x * coarse_x, axis=0, keepdims=True)
    rest = jnp.sum(fine_x * (2.0 * coarse_x + fine_x), axis=0, keepdims=True) + extra
    return (g1, g2, f1, f2), (*split(norm), *split(rest))


meetings = ((0, 0), (0, 1), (1, 0), (1, 1), (0, 2), (2, 0), (1, 2), (2, 1), (0, 3), (3, 0), (1, 3), (3, 1), (2, 2), (2, 3), (3, 2))


def rows_of(pieces, norms, source):
    place = lax.broadcasted_iota(jnp.int32, pieces[0].shape, 0) < 3
    one = jnp.ones_like(norms[0])
    rows = []
    for n, (from_source, from_target) in enumerate(meetings):
        if n >= 2 * len(norms):
            fill = jnp.zeros_like(one)
        elif (n % 2 == 0) == source:
            fill = norms[n // 2]
        else:
            fill = one
        mine = pieces[from_source] if source else -2.0 * pieces[from_target]
        rows.append(jnp.where(place, mine, fill))
    rows.append(jnp.zeros_like(rows[0]))
    return jnp.concatenate(rows, axis=0)


def source_features(block, centre, grid):
    x = coordinates(block, centre)
    features = rows_of(*pieces_of(x, grid, 0.0), True).T.astype(jnp.bfloat16)
    mass = block[3:4]
    place = lax.broadcasted_iota(jnp.int32, block.shape, 0) < 3
    pulls = split(jnp.where(place, x * mass, mass))
    pulls = jnp.concatenate([*pulls, jnp.zeros_like(x)], axis=0).astype(jnp.bfloat16)
    return features, pulls


def target_features(block, centre, grid):
    x = coordinates(block, centre)
    return rows_of(*pieces_of(x, grid, soften), False).astype(jnp.bfloat16)


def pair_pull(source, target, pulls):
    distance = jnp.dot(source, target, preferred_element_type=jnp.float32)
    inverse = lax.rsqrt(jnp.maximum(distance, soften))
    w = inverse * inverse * inverse
    high = w.astype(jnp.bfloat16)
    low = (w - high.astype(jnp.float32)).astype(jnp.bfloat16)
    return jnp.dot(
        jnp.concatenate([pulls, pulls], axis=1),
        jnp.concatenate([high, low], axis=0),
        preferred_element_type=jnp.float32,
    )


def running_count(chosen):
    rows, lanes = chosen.shape
    before = lax.broadcasted_iota(jnp.int32, (lanes, lanes), 0) <= lax.broadcasted_iota(jnp.int32, (lanes, lanes), 1)
    running = jnp.dot(
        jnp.where(chosen, 1.0, 0.0).astype(jnp.bfloat16),
        jnp.where(before, 1.0, 0.0).astype(jnp.bfloat16),
        preferred_element_type=jnp.float32,
    )
    ends = running[:, lanes - 1 : lanes]
    earlier = lax.broadcasted_iota(jnp.int32, (rows, rows), 1) < lax.broadcasted_iota(jnp.int32, (rows, rows), 0)
    offsets = jnp.dot(
        jnp.where(earlier, 1.0, 0.0).astype(jnp.bfloat16),
        jnp.broadcast_to(ends, (rows, lanes)).astype(jnp.bfloat16),
        preferred_element_type=jnp.float32,
    )
    return running + offsets, jnp.sum(ends, axis=0, keepdims=True)


def order_pairs(coded, radix, departures, own_blocks):
    rows, lanes = coded.shape
    total = rows * lanes
    place = lanes * lax.broadcasted_iota(jnp.int32, (rows, lanes), 0) + lax.broadcasted_iota(jnp.int32, (rows, lanes), 1)
    live = coded >= 0
    coded = jnp.maximum(coded, 0)
    pair_targets = coded // radix
    pair_sources = coded % radix
    own = live & (pair_sources < own_blocks)
    leaves = pair_targets == departures[0]
    for d in departures[1:]:
        leaves = leaves | (pair_targets == d)
    leaves = live & leaves & ~own
    own_count, own_total = running_count(own)
    leave_count, leave_total = running_count(leaves)
    slot = jnp.where(
        own,
        own_count - 1.0,
        jnp.where(
            leaves,
            own_total + leave_count - 1.0,
            own_total + leave_total + place.astype(jnp.float32) - own_count - leave_count,
        ),
    ).T
    digits = []
    for values in (pair_targets, pair_sources):
        digits += [(values // 128).astype(jnp.float32), (values % 128).astype(jnp.float32)]
    moved = jnp.zeros((8, total), jnp.float32)
    lane = lax.broadcasted_iota(jnp.int32, (lanes, total), 1).astype(jnp.float32)
    for r in range(rows):
        values = jnp.concatenate([d[r : r + 1] for d in digits] + [jnp.zeros((4, lanes), jnp.float32)], axis=0)
        here = jnp.where(slot[:, r : r + 1] == lane, 1.0, 0.0).astype(jnp.bfloat16)
        moved = moved + jnp.dot(values.astype(jnp.bfloat16), here, preferred_element_type=jnp.float32)
    targets = 128.0 * moved[0:1] + moved[1:2]
    sources = 128.0 * moved[2:3] + moved[3:4]
    live_total = jnp.sum(jnp.where(live, 1.0, 0.0), axis=1, keepdims=True)
    return targets, sources, own_total, leave_total, jnp.sum(live_total, axis=0, keepdims=True)


def early_groups(steps, limit):
    plan = []
    for k, (axis, stride) in enumerate(steps):
        groups = 0 if k == 1 else 1 if (axis, stride) == ("gz", 1) else 2
        plan.append(min(groups, limit - sum(plan)))
    return plan


def exchange_kernel(
    steps,
    plan,
    unroll,
    radix,
    coded_ref,
    select_vmem,
    moves_vmem,
    bodies_ref,
    pool_ref,
    sums_ref,
    order_ref,
    sources,
    pulls,
    targets,
    outgoing,
    arriving,
    passed,
    chosen_vmem,
    chosen_ref,
    parts,
    order,
    select_ref,
    moves_ref,
    send_sem,
    recv_sem,
    load_sem,
):
    own_blocks = bodies_ref.shape[0]
    send_count = outgoing.shape[1]
    partners = []
    for axis, stride in steps:
        me = lax.axis_index(axis)
        side = lax.rem(me // stride, 2)
        partners.append({axis: me + (1 - 2 * side) * stride})
    across = dict(partners[0])
    for axis, place in partners[1].items():
        across[axis] = across[axis] + place - lax.axis_index(axis) if axis in across else place
    barrier = pltpu.get_barrier_semaphore()
    for partner in [*partners, across]:
        pl.semaphore_signal(
            barrier, inc=1, device_id=partner, device_id_type=pl.DeviceIdType.MESH
        )
    load_select = pltpu.make_async_copy(select_vmem, select_ref, load_sem.at[0])
    load_moves = pltpu.make_async_copy(moves_vmem, moves_ref, load_sem.at[1])
    load_select.start()
    load_moves.start()
    pool_ref[0:own_blocks] = bodies_ref[...]
    centre, grid = frame_of(bodies_ref)
    batch = math.gcd(own_blocks, 12)

    @pl.loop(0, own_blocks // batch)
    def _(group):
        for b in [group * batch + u for u in range(batch)]:
            sources[b], pulls[b] = source_features(bodies_ref[b], centre, grid)
            targets[b] = target_features(bodies_ref[b], centre, grid)

    def remote(source, target, n, partner):
        return pltpu.make_async_remote_copy(
            src_ref=source,
            dst_ref=target,
            send_sem=send_sem.at[n],
            recv_sem=recv_sem.at[n],
            device_id=partner,
            device_id_type=pl.DeviceIdType.MESH,
        )

    hops = len(partners)
    copies = [remote(outgoing.at[k], arriving.at[k], k, partner) for k, partner in enumerate(partners)]
    copies.append(remote(outgoing.at[0], passed, hops, across))
    copies.append(remote(select_vmem.at[1], chosen_vmem, hops + 1, partners[1]))

    def send_first():
        for j in range(send_count):
            outgoing[0, j] = pool_ref[select_ref[0, 0, j]]
            outgoing[1, j] = pool_ref[jnp.minimum(select_ref[1, 0, j], own_blocks - 1)]
        for copy in (copies[0], copies[hops], copies[1], copies[hops + 1]):
            copy.start()

    def send(k):
        for j in range(send_count):
            outgoing[k, j] = pool_ref[select_ref[k, 0, j]]
        copies[k].start()

    def receive(k):
        base = own_blocks + k * send_count
        if k == 1:
            copies[hops + 1].wait_recv()
            load_chosen = pltpu.make_async_copy(chosen_vmem, chosen_ref, load_sem.at[2])
            load_chosen.start()
            for copy in (copies[0], copies[hops], copies[1]):
                copy.wait_recv()
            pool_ref[own_blocks:base] = arriving[0]
            load_chosen.wait()
            for j in range(send_count):
                place = chosen_ref[0, j]
                theirs = passed[jnp.clip(place - own_blocks, 0, send_count - 1)]
                pool_ref[base + j] = jnp.where(place < own_blocks, arriving[1, j], theirs)
        else:
            copies[k].wait_recv()
            pool_ref[base : base + send_count] = arriving[k]

    def prepare(k):
        half = math.gcd(send_count, 8)

        @pl.loop(0, send_count // half)
        def _(group):
            for b in [own_blocks + k * send_count + group * half + u for u in range(half)]:
                sources[b], pulls[b] = source_features(pool_ref[b], centre, grid)

    load_select.wait()
    load_moves.wait()
    pl.semaphore_wait(barrier, len(partners) + 1)
    send_first()
    departures = [moves_ref[0, m] // moves_radix for m in range(moves_ref.shape[1])]
    row_t, row_s, *totals = order_pairs(coded_ref[...], radix, departures, own_blocks)
    own_total = totals[0]
    slots = row_t.shape[1]
    table = [row_t, row_s, *[jnp.broadcast_to(total, row_t.shape) for total in totals]]
    table = jnp.concatenate([*table, jnp.zeros((8 - len(table), slots), jnp.float32)], axis=0)
    order_ref[...] = table.astype(jnp.int32)
    into_order = pltpu.make_async_copy(order_ref, order, load_sem.at[0])
    into_order.start()
    into_order.wait()

    @pl.loop(0, sum(plan))
    def _(group):
        for k in range(2, len(partners)):

            @pl.when(group == sum(plan[:k]))
            def _():
                receive(k - 1)
                send(k)
                if k == 2:
                    prepare(0)
                prepare(k - 1)

        for u in range(unroll):
            p = group * unroll + u
            t = jnp.clip(order[0, p], 0, own_blocks - 1)
            s = jnp.clip(order[1, p], 0, own_blocks - 1)
            pull = pair_pull(sources[s], targets[t], pulls[s])
            pull = pull[0:4] + pull[4:8] + pull[8:12]
            for c in range(4):
                parts[c, pl.ds(p, 1), :] = pull[c : c + 1]

    for k in range(2, len(partners)):
        if sum(plan[:k]) >= sum(plan):
            receive(k - 1)
            send(k)
            if k == 2:
                prepare(0)
            prepare(k - 1)
    early = parts.shape[1]
    members = lax.broadcasted_iota(jnp.int32, (-(-own_blocks // 16) * 16, early), 0)
    spot = lax.broadcasted_iota(jnp.int32, members.shape, 1).astype(jnp.float32)
    chosen = (members == order_ref[0:1, 0:early]) & (spot < own_total)
    chosen = jnp.where(chosen, 1.0, 0.0).astype(jnp.bfloat16)
    for c in range(4):
        total = jnp.zeros((members.shape[0], parts.shape[2]), jnp.float32)
        for piece in split(parts[c]):
            total = total + jnp.dot(chosen, piece.astype(jnp.bfloat16), preferred_element_type=jnp.float32)
        sums_ref[:, c, :] = total[0:own_blocks]
    receive(len(partners) - 1)
    prepare(len(partners) - 1)
    for copy in copies:
        copy.wait_send()


def pull_loop(first, last, order_ref, sources, targets, pulls, sums, unroll):
    slots = order_ref.shape[1]
    nowhere = sums.shape[0] - 1
    wide = 2 * unroll
    whole = jnp.maximum(last - first, 0) // wide

    @pl.loop(0, whole)
    def _(group):
        for u in range(wide):
            p = jnp.minimum(first + group * wide + u, slots - 1)
            t = order_ref[0, p]
            s = order_ref[1, p]
            sums[t] += pair_pull(sources[s], targets[t], pulls[s])

    first = first + whole * wide

    @pl.loop(0, (last - first + unroll - 1) // unroll)
    def _(group):
        for u in range(unroll):
            p = first + group * unroll + u
            live = p < last
            p = jnp.minimum(p, slots - 1)
            t = order_ref[0, p]
            s = order_ref[1, p]
            where = jnp.where(live, t, nowhere)
            sums[where] += pair_pull(sources[s], targets[t], pulls[s])


def update(b, centre, pool_ref, sums, velocity_ref):
    total = sums[b, 0:4] + sums[b, 4:8] + sums[b, 8:12]
    block = pool_ref[b]
    pull = total - coordinates(block, centre) * total[3:4]
    places, velocities = [], []
    for c in range(3):
        velocity_new = velocity_ref[c, pl.ds(b, 1), :] + timestep * pull[c : c + 1]
        velocities.append(velocity_new)
        places.append(block[c : c + 1, :] + timestep * velocity_new)
    return [*places, block[3:4, :], *velocities]


def leaving_range(order_ref, early, unroll):
    first = jnp.minimum(order_ref[2, 0], early)
    groups = (order_ref[2, 0] + order_ref[3, 0] - first + unroll - 1) // unroll
    return first, jnp.minimum(first + groups * unroll, order_ref[4, 0])


def leaving_kernel(
    unroll,
    early,
    order_ref,
    moves_ref,
    pool_ref,
    early_sums_ref,
    velocity_ref,
    sources,
    pulls,
    targets,
    sums,
    *rest,
):
    outboxes, (boxes, used) = rest[:-2], rest[-2:]
    own_blocks = early_sums_ref.shape[0]
    span = pool_ref.shape[2]
    centre, _ = frame_of(pool_ref.at[pl.ds(0, own_blocks)])
    sums[0:own_blocks, 0:4] = early_sums_ref[...]
    sums[0:own_blocks, 4:16] = jnp.zeros((own_blocks, 12, span), jnp.float32)
    sums[own_blocks] = jnp.zeros(sums.shape[1:], jnp.float32)
    boxes[...] = jnp.zeros_like(boxes)
    for g in range(used.shape[0]):
        used[g] = 0
    pull_loop(*leaving_range(order_ref, early, unroll), order_ref, sources, targets, pulls, sums, unroll)
    me = lax.axis_index("gz")
    for m in range(moves_ref.shape[1]):
        owner = moves_ref[0, m] % moves_radix
        slot = used[owner]
        used[owner] = slot + 1
        box = jnp.bitwise_xor(owner, me)
        for c, row in enumerate(update(moves_ref[0, m] // moves_radix, centre, pool_ref, sums, velocity_ref)):
            boxes[box, slot, c : c + 1, :] = row
    for g, outbox in enumerate(outboxes):
        outbox[...] = boxes[g]


def staying_kernel(
    unroll,
    early,
    order_ref,
    moves_ref,
    pool_ref,
    sums_ref,
    velocity_ref,
    sources,
    pulls,
    targets,
    resident_ref,
    sums,
):
    own_blocks = sums_ref.shape[0] - 1
    span = pool_ref.shape[2]
    centre, _ = frame_of(pool_ref.at[pl.ds(0, own_blocks)])
    sums[...] = sums_ref[...]
    _, first = leaving_range(order_ref, early, unroll)
    pull_loop(first, order_ref[4, 0], order_ref, sources, targets, pulls, sums, unroll)
    batch = math.gcd(own_blocks, 12)

    @pl.loop(0, own_blocks // batch)
    def _(group):
        for b in [group * batch + u for u in range(batch)]:
            for c, row in enumerate(update(b, centre, pool_ref, sums, velocity_ref)):
                resident_ref[c, pl.ds(b, 1), :] = row

    for m in range(moves_ref.shape[1]):
        for c in range(resident_ref.shape[0]):
            resident_ref[c, pl.ds(moves_ref[0, m] // moves_radix, 1), :] = jnp.zeros((1, span), jnp.float32)


def inbox_kernel(*refs):
    boxes, moved_ref = refs[:-1], refs[-1]
    me = lax.axis_index("gz")
    slot_total = boxes[0].shape[0]
    for g, box in enumerate(boxes):
        sender = jnp.bitwise_xor(me, g)
        for slot in range(slot_total):
            for c in range(moved_ref.shape[0]):
                moved_ref[c, pl.ds(sender * slot_total + slot, 1), :] = box[slot, c : c + 1, :]


def on_device(bodies, velocity, select, pair_target, pair_source, counts, departures, owners):
    own_blocks = bodies.shape[0]
    span = bodies.shape[2]
    smem = pl.BlockSpec(memory_space=pltpu.SMEM)
    vmem = pl.BlockSpec(memory_space=pltpu.VMEM)
    steps = [
        (axis, 2**bit)
        for axis in ("gx", "gy", "gz")
        for bit in range(lax.axis_size(axis).bit_length() - 1)
    ]
    send_count = select.shape[2]
    slab = pltpu.VMEM((len(steps), send_count, 4, span), jnp.float32)
    slots = pair_target.shape[1]
    unroll = math.gcd(slots, deepest_unroll)
    plan = early_groups(steps, slots // unroll)
    early = sum(plan) * unroll
    pool_size = own_blocks + len(steps) * send_count
    move_count = departures.shape[1]
    radix = 1 << (pool_size - 1).bit_length()
    place = lax.broadcasted_iota(jnp.int32, pair_target.shape, 1)
    coded = jnp.where(place < counts[None, :], pair_target * radix + pair_source, -1).reshape(slots // 128, 128)
    moves = departures * moves_radix + jnp.transpose(owners, (1, 0))
    velocity = jnp.transpose(velocity, (1, 0, 2))
    pool, early_sums, order, sources, pulls, targets = pl.pallas_call(
        functools.partial(exchange_kernel, steps, plan, unroll, radix),
        out_shape=(
            jax.ShapeDtypeStruct((pool_size, 4, span), jnp.float32),
            jax.ShapeDtypeStruct((own_blocks, 4, span), jnp.float32),
            jax.ShapeDtypeStruct((8, slots), jnp.int32),
            jax.ShapeDtypeStruct((pool_size, span, 64), jnp.bfloat16),
            jax.ShapeDtypeStruct((pool_size, 16, span), jnp.bfloat16),
            jax.ShapeDtypeStruct((own_blocks, 64, span), jnp.bfloat16),
        ),
        in_specs=[vmem] * 4,
        out_specs=(vmem,) * 6,
        scratch_shapes=[
            slab,
            slab,
            pltpu.VMEM((send_count, 4, span), jnp.float32),
            pltpu.VMEM((1, send_count), jnp.int32),
            pltpu.SMEM((1, send_count), jnp.int32),
            pltpu.VMEM((4, early, span), jnp.float32),
            pltpu.SMEM((8, slots), jnp.int32),
            pltpu.SMEM((len(steps), 1, send_count), jnp.int32),
            pltpu.SMEM((1, move_count), jnp.int32),
            pltpu.SemaphoreType.DMA((len(steps) + 2,)),
            pltpu.SemaphoreType.DMA((len(steps) + 2,)),
            pltpu.SemaphoreType.DMA((3,)),
        ],
        compiler_params=pltpu.CompilerParams(
            collective_id=0, has_side_effects=True, vmem_limit_bytes=32 << 20
        ),
        cost_estimate=pl.CostEstimate(flops=10**10, bytes_accessed=1048576, transcendentals=0),
        name="exchange",
    )(coded, jnp.transpose(select, (1, 0, 2)), moves, bodies)
    group_size = lax.axis_size("gz")
    slot_total = max(2, 2 * move_count // group_size)
    work = pl.CostEstimate(flops=20 * slots // 4 * span * span, bytes_accessed=1 << 20, transcendentals=0)
    box = jax.ShapeDtypeStruct((slot_total, 7, span), jnp.float32)
    sums, *outboxes = pl.pallas_call(
        functools.partial(leaving_kernel, unroll, early),
        out_shape=(jax.ShapeDtypeStruct((own_blocks + 1, 16, span), jnp.float32),) + (box,) * group_size,
        in_specs=[smem, smem] + [vmem] * 6,
        out_specs=(vmem,) * (1 + group_size),
        scratch_shapes=[
            pltpu.VMEM((group_size, slot_total, 7, span), jnp.float32),
            pltpu.SMEM((group_size,), jnp.int32),
        ],
        compiler_params=pltpu.CompilerParams(vmem_limit_bytes=24 << 20),
        name="leaving",
    )(order, moves, pool, early_sums, velocity, sources, pulls, targets)
    inboxes = [outboxes[0]]
    for g in range(1, group_size):
        pairs = [(i, i ^ g) for i in range(group_size)]
        inboxes.append(lax.ppermute(outboxes[g], "gz", pairs))
    resident = pl.pallas_call(
        functools.partial(staying_kernel, unroll, early),
        out_shape=jax.ShapeDtypeStruct((7, own_blocks, span), jnp.float32),
        in_specs=[smem, smem] + [vmem] * 6,
        out_specs=vmem,
        scratch_shapes=[pltpu.VMEM((own_blocks + 1, 16, span), jnp.float32)],
        compiler_params=pltpu.CompilerParams(vmem_limit_bytes=24 << 20),
        cost_estimate=work,
        name="staying",
    )(order, moves, pool, sums, velocity, sources, pulls, targets)
    moved = pl.pallas_call(
        inbox_kernel,
        out_shape=jax.ShapeDtypeStruct((7, group_size * slot_total, span), jnp.float32),
        in_specs=[vmem] * group_size,
        out_specs=vmem,
        compiler_params=pltpu.CompilerParams(vmem_limit_bytes=16 << 20),
        name="inbox",
    )(*inboxes)
    return jnp.transpose(resident, (1, 0, 2)), jnp.transpose(moved, (1, 0, 2))


def solution(mesh):
    everywhere = ("gx", "gy", "gz")
    cube = P(everywhere, None, None)
    flat = P(everywhere, None)
    return jax.shard_map(
        on_device,
        mesh=mesh,
        in_specs=(cube, cube, cube, flat, flat, P(everywhere), flat, flat),
        out_specs=(cube, cube),
        check_vma=False,
    )
```

```python
import functools
import math

import jax
import jax.numpy as jnp
from jax import lax
from jax.experimental import pallas as pl
from jax.experimental.pallas import tpu as pltpu
from jax.sharding import PartitionSpec as P

soften = 0.01
timestep = 0.25
deepest_unroll = 64
moves_radix = 1 << 16
coarse = 2.0**14.5


def split(values):
    high = values.astype(jnp.bfloat16).astype(jnp.float32)
    rest = values - high
    middle = rest.astype(jnp.bfloat16).astype(jnp.float32)
    return high, middle, rest - middle


def frame_of(own_ref):
    lowest = jnp.min(own_ref[...], axis=0)
    highest = jnp.max(own_ref[...], axis=0)
    lowest = jnp.min(lowest, axis=1, keepdims=True)
    highest = jnp.max(highest, axis=1, keepdims=True)
    place = lax.broadcasted_iota(jnp.int32, lowest.shape, 0) < 3
    centre = jnp.where(place, 0.5 * lowest + 0.5 * highest, 0.0)
    reach = jnp.where(place, 0.5 * highest - 0.5 * lowest, 0.0)
    reach = jnp.max(reach, axis=0, keepdims=True)
    return centre, reach * coarse


def coordinates(block, centre):
    place = lax.broadcasted_iota(jnp.int32, block.shape, 0) < 3
    return jnp.where(place, block - centre, 0.0)


def pieces_of(x, grid, extra):
    coarse_x = (x + grid) - grid
    fine_x = x - coarse_x
    g1 = coarse_x.astype(jnp.bfloat16).astype(jnp.float32)
    g2 = coarse_x - g1
    f1 = fine_x.astype(jnp.bfloat16).astype(jnp.float32)
    f2 = fine_x - f1
    norm = jnp.sum(coarse_x * coarse_x, axis=0, keepdims=True)
    rest = jnp.sum(fine_x * (2.0 * coarse_x + fine_x), axis=0, keepdims=True) + extra
    return (g1, g2, f1, f2), (*split(norm), *split(rest))


meetings = ((0, 0), (0, 1), (1, 0), (1, 1), (0, 2), (2, 0), (1, 2), (2, 1), (0, 3), (3, 0), (1, 3), (3, 1), (2, 2), (2, 3), (3, 2))


def rows_of(pieces, norms, source):
    place = lax.broadcasted_iota(jnp.int32, pieces[0].shape, 0) < 3
    one = jnp.ones_like(norms[0])
    rows = []
    for n, (from_source, from_target) in enumerate(meetings):
        if n >= 2 * len(norms):
            fill = jnp.zeros_like(one)
        elif (n % 2 == 0) == source:
            fill = norms[n // 2]
        else:
            fill = one
        mine = pieces[from_source] if source else -2.0 * pieces[from_target]
        rows.append(jnp.where(place, mine, fill))
    rows.append(jnp.zeros_like(rows[0]))
    return jnp.concatenate(rows, axis=0)


def source_features(block, centre, grid):
    x = coordinates(block, centre)
    features = rows_of(*pieces_of(x, grid, 0.0), True).T.astype(jnp.bfloat16)
    mass = block[3:4]
    place = lax.broadcasted_iota(jnp.int32, block.shape, 0) < 3
    pulls = split(jnp.where(place, x * mass, mass))
    pulls = jnp.concatenate([*pulls, jnp.zeros_like(x)], axis=0).astype(jnp.bfloat16)
    return features, pulls


def target_features(block, centre, grid):
    x = coordinates(block, centre)
    return rows_of(*pieces_of(x, grid, soften), False).astype(jnp.bfloat16)


def pair_pull(source, target, pulls):
    distance = jnp.dot(source, target, preferred_element_type=jnp.float32)
    inverse = lax.rsqrt(jnp.maximum(distance, soften))
    w = inverse * inverse * inverse
    high = w.astype(jnp.bfloat16)
    low = (w - high.astype(jnp.float32)).astype(jnp.bfloat16)
    return jnp.dot(
        jnp.concatenate([pulls, pulls], axis=1),
        jnp.concatenate([high, low], axis=0),
        preferred_element_type=jnp.float32,
    )


def running_count(chosen):
    rows, lanes = chosen.shape
    before = lax.broadcasted_iota(jnp.int32, (lanes, lanes), 0) <= lax.broadcasted_iota(jnp.int32, (lanes, lanes), 1)
    running = jnp.dot(
        jnp.where(chosen, 1.0, 0.0).astype(jnp.bfloat16),
        jnp.where(before, 1.0, 0.0).astype(jnp.bfloat16),
        preferred_element_type=jnp.float32,
    )
    ends = running[:, lanes - 1 : lanes]
    earlier = lax.broadcasted_iota(jnp.int32, (rows, rows), 1) < lax.broadcasted_iota(jnp.int32, (rows, rows), 0)
    offsets = jnp.dot(
        jnp.where(earlier, 1.0, 0.0).astype(jnp.bfloat16),
        jnp.broadcast_to(ends, (rows, lanes)).astype(jnp.bfloat16),
        preferred_element_type=jnp.float32,
    )
    return running + offsets, jnp.sum(ends, axis=0, keepdims=True)


def order_pairs(coded, radix, departures, own_blocks):
    rows, lanes = coded.shape
    total = rows * lanes
    place = lanes * lax.broadcasted_iota(jnp.int32, (rows, lanes), 0) + lax.broadcasted_iota(jnp.int32, (rows, lanes), 1)
    live = coded >= 0
    coded = jnp.maximum(coded, 0)
    pair_targets = coded // radix
    pair_sources = coded % radix
    own = live & (pair_sources < own_blocks)
    leaves = pair_targets == departures[0]
    for d in departures[1:]:
        leaves = leaves | (pair_targets == d)
    leaves = live & leaves & ~own
    own_count, own_total = running_count(own)
    leave_count, leave_total = running_count(leaves)
    slot = jnp.where(
        own,
        own_count - 1.0,
        jnp.where(
            leaves,
            own_total + leave_count - 1.0,
            own_total + leave_total + place.astype(jnp.float32) - own_count - leave_count,
        ),
    ).T
    digits = []
    for values in (pair_targets, pair_sources):
        digits += [(values // 128).astype(jnp.float32), (values % 128).astype(jnp.float32)]
    moved = jnp.zeros((8, total), jnp.float32)
    lane = lax.broadcasted_iota(jnp.int32, (lanes, total), 1).astype(jnp.float32)
    for r in range(rows):
        values = jnp.concatenate([d[r : r + 1] for d in digits] + [jnp.zeros((4, lanes), jnp.float32)], axis=0)
        here = jnp.where(slot[:, r : r + 1] == lane, 1.0, 0.0).astype(jnp.bfloat16)
        moved = moved + jnp.dot(values.astype(jnp.bfloat16), here, preferred_element_type=jnp.float32)
    targets = 128.0 * moved[0:1] + moved[1:2]
    sources = 128.0 * moved[2:3] + moved[3:4]
    live_total = jnp.sum(jnp.where(live, 1.0, 0.0), axis=1, keepdims=True)
    return targets, sources, own_total, leave_total, jnp.sum(live_total, axis=0, keepdims=True)


def early_groups(steps, limit):
    plan = []
    for k, (axis, stride) in enumerate(steps):
        groups = 0 if k == 1 else 1 if (axis, stride) == ("gz", 1) else 2
        plan.append(min(groups, limit - sum(plan)))
    return plan


def exchange_kernel(
    steps,
    plan,
    unroll,
    radix,
    coded_ref,
    select_vmem,
    moves_vmem,
    bodies_ref,
    pool_ref,
    sums_ref,
    order_ref,
    sources,
    pulls,
    targets,
    outgoing,
    arriving,
    passed,
    chosen_vmem,
    chosen_ref,
    parts,
    order,
    select_ref,
    moves_ref,
    send_sem,
    recv_sem,
    load_sem,
):
    own_blocks = bodies_ref.shape[0]
    send_count = outgoing.shape[1]
    partners = []
    for axis, stride in steps:
        me = lax.axis_index(axis)
        side = lax.rem(me // stride, 2)
        partners.append({axis: me + (1 - 2 * side) * stride})
    across = dict(partners[0])
    for axis, place in partners[1].items():
        across[axis] = across[axis] + place - lax.axis_index(axis) if axis in across else place
    barrier = pltpu.get_barrier_semaphore()
    for partner in [*partners, across]:
        pl.semaphore_signal(
            barrier, inc=1, device_id=partner, device_id_type=pl.DeviceIdType.MESH
        )
    load_select = pltpu.make_async_copy(select_vmem, select_ref, load_sem.at[0])
    load_moves = pltpu.make_async_copy(moves_vmem, moves_ref, load_sem.at[1])
    load_select.start()
    load_moves.start()
    pool_ref[0:own_blocks] = bodies_ref[...]
    centre, grid = frame_of(bodies_ref)
    batch = math.gcd(own_blocks, 12)

    @pl.loop(0, own_blocks // batch)
    def _(group):
        for b in [group * batch + u for u in range(batch)]:
            sources[b], pulls[b] = source_features(bodies_ref[b], centre, grid)
            targets[b] = target_features(bodies_ref[b], centre, grid)

    def remote(source, target, n, partner):
        return pltpu.make_async_remote_copy(
            src_ref=source,
            dst_ref=target,
            send_sem=send_sem.at[n],
            recv_sem=recv_sem.at[n],
            device_id=partner,
            device_id_type=pl.DeviceIdType.MESH,
        )

    hops = len(partners)
    copies = [remote(outgoing.at[k], arriving.at[k], k, partner) for k, partner in enumerate(partners)]
    copies.append(remote(outgoing.at[0], passed, hops, across))
    copies.append(remote(select_vmem.at[1], chosen_vmem, hops + 1, partners[1]))

    def send_first():
        for j in range(send_count):
            outgoing[0, j] = pool_ref[select_ref[0, 0, j]]
            outgoing[1, j] = pool_ref[jnp.minimum(select_ref[1, 0, j], own_blocks - 1)]
        for copy in (copies[0], copies[hops], copies[1], copies[hops + 1]):
            copy.start()

    def send(k):
        for j in range(send_count):
            outgoing[k, j] = pool_ref[select_ref[k, 0, j]]
        copies[k].start()

    def receive(k):
        base = own_blocks + k * send_count
        if k == 1:
            copies[hops + 1].wait_recv()
            load_chosen = pltpu.make_async_copy(chosen_vmem, chosen_ref, load_sem.at[2])
            load_chosen.start()
            for copy in (copies[0], copies[hops], copies[1]):
                copy.wait_recv()
            pool_ref[own_blocks:base] = arriving[0]
            load_chosen.wait()
            for j in range(send_count):
                place = chosen_ref[0, j]
                theirs = passed[jnp.clip(place - own_blocks, 0, send_count - 1)]
                pool_ref[base + j] = jnp.where(place < own_blocks, arriving[1, j], theirs)
        else:
            copies[k].wait_recv()
            pool_ref[base : base + send_count] = arriving[k]

    def prepare(k):
        half = math.gcd(send_count, 8)

        @pl.loop(0, send_count // half)
        def _(group):
            for b in [own_blocks + k * send_count + group * half + u for u in range(half)]:
                sources[b], pulls[b] = source_features(pool_ref[b], centre, grid)

    load_select.wait()
    load_moves.wait()
    pl.semaphore_wait(barrier, len(partners) + 1)
    send_first()
    departures = [moves_ref[0, m] // moves_radix for m in range(moves_ref.shape[1])]
    row_t, row_s, *totals = order_pairs(coded_ref[...], radix, departures, own_blocks)
    own_total = totals[0]
    slots = row_t.shape[1]
    table = [row_t, row_s, *[jnp.broadcast_to(total, row_t.shape) for total in totals]]
    table = jnp.concatenate([*table, jnp.zeros((8 - len(table), slots), jnp.float32)], axis=0)
    order_ref[...] = table.astype(jnp.int32)
    into_order = pltpu.make_async_copy(order_ref, order, load_sem.at[0])
    into_order.start()
    into_order.wait()

    @pl.loop(0, sum(plan))
    def _(group):
        for k in range(2, len(partners)):

            @pl.when(group == sum(plan[:k]))
            def _():
                receive(k - 1)
                send(k)
                if k == 2:
                    prepare(0)
                prepare(k - 1)

        for u in range(unroll):
            p = group * unroll + u
            t = jnp.clip(order[0, p], 0, own_blocks - 1)
            s = jnp.clip(order[1, p], 0, own_blocks - 1)
            pull = pair_pull(sources[s], targets[t], pulls[s])
            pull = pull[0:4] + pull[4:8] + pull[8:12]
            for c in range(4):
                parts[c, pl.ds(p, 1), :] = pull[c : c + 1]

    for k in range(2, len(partners)):
        if sum(plan[:k]) >= sum(plan):
            receive(k - 1)
            send(k)
            if k == 2:
                prepare(0)
            prepare(k - 1)
    early = parts.shape[1]
    members = lax.broadcasted_iota(jnp.int32, (-(-own_blocks // 16) * 16, early), 0)
    spot = lax.broadcasted_iota(jnp.int32, members.shape, 1).astype(jnp.float32)
    chosen = (members == order_ref[0:1, 0:early]) & (spot < own_total)
    chosen = jnp.where(chosen, 1.0, 0.0).astype(jnp.bfloat16)
    for c in range(4):
        total = jnp.zeros((members.shape[0], parts.shape[2]), jnp.float32)
        for piece in split(parts[c]):
            total = total + jnp.dot(chosen, piece.astype(jnp.bfloat16), preferred_element_type=jnp.float32)
        sums_ref[:, c, :] = total[0:own_blocks]
    receive(len(partners) - 1)
    prepare(len(partners) - 1)
    for copy in copies:
        copy.wait_send()


def pull_loop(first, last, order_ref, sources, targets, pulls, sums, unroll):
    slots = order_ref.shape[1]
    nowhere = sums.shape[0] - 1
    wide = 4 * unroll
    whole = jnp.maximum(last - first, 0) // wide

    @pl.loop(0, whole)
    def _(group):
        for u in range(wide):
            p = jnp.minimum(first + group * wide + u, slots - 1)
            t = order_ref[0, p]
            s = order_ref[1, p]
            sums[t] += pair_pull(sources[s], targets[t], pulls[s])

    first = first + whole * wide

    @pl.loop(0, (last - first + unroll - 1) // unroll)
    def _(group):
        for u in range(unroll):
            p = first + group * unroll + u
            live = p < last
            p = jnp.minimum(p, slots - 1)
            t = order_ref[0, p]
            s = order_ref[1, p]
            where = jnp.where(live, t, nowhere)
            sums[where] += pair_pull(sources[s], targets[t], pulls[s])


def update(b, centre, pool_ref, sums, velocity_ref):
    total = sums[b, 0:4] + sums[b, 4:8] + sums[b, 8:12]
    block = pool_ref[b]
    pull = total - coordinates(block, centre) * total[3:4]
    places, velocities = [], []
    for c in range(3):
        velocity_new = velocity_ref[c, pl.ds(b, 1), :] + timestep * pull[c : c + 1]
        velocities.append(velocity_new)
        places.append(block[c : c + 1, :] + timestep * velocity_new)
    return [*places, block[3:4, :], *velocities]


def leaving_range(order_ref, early, unroll):
    first = jnp.minimum(order_ref[2, 0], early)
    groups = (order_ref[2, 0] + order_ref[3, 0] - first + unroll - 1) // unroll
    return first, jnp.minimum(first + groups * unroll, order_ref[4, 0])


def leaving_kernel(
    unroll,
    early,
    order_ref,
    moves_ref,
    pool_ref,
    early_sums_ref,
    velocity_ref,
    sources,
    pulls,
    targets,
    sums,
    *rest,
):
    outboxes, (boxes, used) = rest[:-2], rest[-2:]
    own_blocks = early_sums_ref.shape[0]
    span = pool_ref.shape[2]
    centre, _ = frame_of(pool_ref.at[pl.ds(0, own_blocks)])
    sums[0:own_blocks, 0:4] = early_sums_ref[...]
    sums[0:own_blocks, 4:16] = jnp.zeros((own_blocks, 12, span), jnp.float32)
    sums[own_blocks] = jnp.zeros(sums.shape[1:], jnp.float32)
    boxes[...] = jnp.zeros_like(boxes)
    for g in range(used.shape[0]):
        used[g] = 0
    pull_loop(*leaving_range(order_ref, early, unroll), order_ref, sources, targets, pulls, sums, unroll)
    me = lax.axis_index("gz")
    for m in range(moves_ref.shape[1]):
        owner = moves_ref[0, m] % moves_radix
        slot = used[owner]
        used[owner] = slot + 1
        box = jnp.bitwise_xor(owner, me)
        for c, row in enumerate(update(moves_ref[0, m] // moves_radix, centre, pool_ref, sums, velocity_ref)):
            boxes[box, slot, c : c + 1, :] = row
    for g, outbox in enumerate(outboxes):
        outbox[...] = boxes[g]


def staying_kernel(
    unroll,
    early,
    order_ref,
    moves_ref,
    pool_ref,
    sums_ref,
    velocity_ref,
    sources,
    pulls,
    targets,
    resident_ref,
    sums,
):
    own_blocks = sums_ref.shape[0] - 1
    span = pool_ref.shape[2]
    centre, _ = frame_of(pool_ref.at[pl.ds(0, own_blocks)])
    sums[...] = sums_ref[...]
    _, first = leaving_range(order_ref, early, unroll)
    pull_loop(first, order_ref[4, 0], order_ref, sources, targets, pulls, sums, unroll)
    batch = math.gcd(own_blocks, 12)

    @pl.loop(0, own_blocks // batch)
    def _(group):
        for b in [group * batch + u for u in range(batch)]:
            for c, row in enumerate(update(b, centre, pool_ref, sums, velocity_ref)):
                resident_ref[c, pl.ds(b, 1), :] = row

    for m in range(moves_ref.shape[1]):
        for c in range(resident_ref.shape[0]):
            resident_ref[c, pl.ds(moves_ref[0, m] // moves_radix, 1), :] = jnp.zeros((1, span), jnp.float32)


def inbox_kernel(*refs):
    boxes, moved_ref = refs[:-1], refs[-1]
    me = lax.axis_index("gz")
    slot_total = boxes[0].shape[0]
    for g, box in enumerate(boxes):
        sender = jnp.bitwise_xor(me, g)
        for slot in range(slot_total):
            for c in range(moved_ref.shape[0]):
                moved_ref[c, pl.ds(sender * slot_total + slot, 1), :] = box[slot, c : c + 1, :]


def on_device(bodies, velocity, select, pair_target, pair_source, counts, departures, owners):
    own_blocks = bodies.shape[0]
    span = bodies.shape[2]
    smem = pl.BlockSpec(memory_space=pltpu.SMEM)
    vmem = pl.BlockSpec(memory_space=pltpu.VMEM)
    steps = [
        (axis, 2**bit)
        for axis in ("gx", "gy", "gz")
        for bit in range(lax.axis_size(axis).bit_length() - 1)
    ]
    send_count = select.shape[2]
    slab = pltpu.VMEM((len(steps), send_count, 4, span), jnp.float32)
    slots = pair_target.shape[1]
    unroll = math.gcd(slots, deepest_unroll)
    plan = early_groups(steps, slots // unroll)
    early = sum(plan) * unroll
    pool_size = own_blocks + len(steps) * send_count
    move_count = departures.shape[1]
    radix = 1 << (pool_size - 1).bit_length()
    place = lax.broadcasted_iota(jnp.int32, pair_target.shape, 1)
    coded = jnp.where(place < counts[None, :], pair_target * radix + pair_source, -1).reshape(slots // 128, 128)
    moves = departures * moves_radix + jnp.transpose(owners, (1, 0))
    velocity = jnp.transpose(velocity, (1, 0, 2))
    pool, early_sums, order, sources, pulls, targets = pl.pallas_call(
        functools.partial(exchange_kernel, steps, plan, unroll, radix),
        out_shape=(
            jax.ShapeDtypeStruct((pool_size, 4, span), jnp.float32),
            jax.ShapeDtypeStruct((own_blocks, 4, span), jnp.float32),
            jax.ShapeDtypeStruct((8, slots), jnp.int32),
            jax.ShapeDtypeStruct((pool_size, span, 64), jnp.bfloat16),
            jax.ShapeDtypeStruct((pool_size, 16, span), jnp.bfloat16),
            jax.ShapeDtypeStruct((own_blocks, 64, span), jnp.bfloat16),
        ),
        in_specs=[vmem] * 4,
        out_specs=(vmem,) * 6,
        scratch_shapes=[
            slab,
            slab,
            pltpu.VMEM((send_count, 4, span), jnp.float32),
            pltpu.VMEM((1, send_count), jnp.int32),
            pltpu.SMEM((1, send_count), jnp.int32),
            pltpu.VMEM((4, early, span), jnp.float32),
            pltpu.SMEM((8, slots), jnp.int32),
            pltpu.SMEM((len(steps), 1, send_count), jnp.int32),
            pltpu.SMEM((1, move_count), jnp.int32),
            pltpu.SemaphoreType.DMA((len(steps) + 2,)),
            pltpu.SemaphoreType.DMA((len(steps) + 2,)),
            pltpu.SemaphoreType.DMA((3,)),
        ],
        compiler_params=pltpu.CompilerParams(
            collective_id=0, has_side_effects=True, vmem_limit_bytes=32 << 20
        ),
        cost_estimate=pl.CostEstimate(flops=10**10, bytes_accessed=1048576, transcendentals=0),
        name="exchange",
    )(coded, jnp.transpose(select, (1, 0, 2)), moves, bodies)
    group_size = lax.axis_size("gz")
    slot_total = max(2, 2 * move_count // group_size)
    work = pl.CostEstimate(flops=20 * slots // 4 * span * span, bytes_accessed=1 << 20, transcendentals=0)
    box = jax.ShapeDtypeStruct((slot_total, 7, span), jnp.float32)
    sums, *outboxes = pl.pallas_call(
        functools.partial(leaving_kernel, unroll // 2, early),
        out_shape=(jax.ShapeDtypeStruct((own_blocks + 1, 16, span), jnp.float32),) + (box,) * group_size,
        in_specs=[smem, smem] + [vmem] * 6,
        out_specs=(vmem,) * (1 + group_size),
        scratch_shapes=[
            pltpu.VMEM((group_size, slot_total, 7, span), jnp.float32),
            pltpu.SMEM((group_size,), jnp.int32),
        ],
        compiler_params=pltpu.CompilerParams(vmem_limit_bytes=24 << 20),
        name="leaving",
    )(order, moves, pool, early_sums, velocity, sources, pulls, targets)
    inboxes = [outboxes[0]]
    for g in range(1, group_size):
        pairs = [(i, i ^ g) for i in range(group_size)]
        inboxes.append(lax.ppermute(outboxes[g], "gz", pairs))
    resident = pl.pallas_call(
        functools.partial(staying_kernel, unroll // 2, early),
        out_shape=jax.ShapeDtypeStruct((7, own_blocks, span), jnp.float32),
        in_specs=[smem, smem] + [vmem] * 6,
        out_specs=vmem,
        scratch_shapes=[pltpu.VMEM((own_blocks + 1, 16, span), jnp.float32)],
        compiler_params=pltpu.CompilerParams(vmem_limit_bytes=24 << 20),
        cost_estimate=work,
        name="staying",
    )(order, moves, pool, sums, velocity, sources, pulls, targets)
    moved = pl.pallas_call(
        inbox_kernel,
        out_shape=jax.ShapeDtypeStruct((7, group_size * slot_total, span), jnp.float32),
        in_specs=[vmem] * group_size,
        out_specs=vmem,
        compiler_params=pltpu.CompilerParams(vmem_limit_bytes=16 << 20),
        name="inbox",
    )(*inboxes)
    return jnp.transpose(resident, (1, 0, 2)), jnp.transpose(moved, (1, 0, 2))


def solution(mesh):
    everywhere = ("gx", "gy", "gz")
    cube = P(everywhere, None, None)
    flat = P(everywhere, None)
    return jax.shard_map(
        on_device,
        mesh=mesh,
        in_specs=(cube, cube, cube, flat, flat, P(everywhere), flat, flat),
        out_specs=(cube, cube),
        check_vma=False,
    )
```
